32 devices in a mesh: chan: 4 (over y, x), facet: 8 (over z, core).
Axes of the slice: x: 2, y: 2, z: 4, core: 2. Of those that a mesh axis runs over, the one named last changes fastest.
Arguments:
- image_field: float32 [4, 2048, 2048], P('chan', 'facet'), may hold values from -6 to 6
- weights: bfloat16 [4, 2048, 2048], P('chan', None, 'facet'), may hold values from 0.049804688 to 1
- measured: bfloat16 [4, 2, 2048, 2048], P('chan', None, None, 'facet'), may hold values from -6 to 6
- dual_field: bfloat16 [4, 2, 2048, 2048], P(None, None, 'facet', 'chan'), may hold values from -3 to 3
Outputs:
- image_next: float32 [4, 2048, 2048], P(None, 'facet', 'chan')
- dual_next: bfloat16 [4, 2, 2048, 2048], P(None, None, 'facet', 'chan')
The draws below stay inside these ranges and needn't reach their ends.
All inputs are finite; a program needn't handle non-finite values.
Results may differ from the reference program's by a relative error of at most 0.001.
Values sent between devices are 32-bit elements; how exact they have to be, the bound alone decides.
A program may use at most 128 MiB of HBM per device.

```python
import math
import jax
import jax.numpy as jnp
from jax import lax

GRID = 2048
CHANNELS = 4


def block_levels(key, dims, split, low, top_value):
    loudness = 1.0
    for axis_at, shards_of in split:
        steps = jax.random.uniform(jax.random.fold_in(jax.random.fold_in(key, 6), axis_at), (shards_of,), jnp.float32, low / len(split), top_value / len(split))
        loudness = loudness * jnp.repeat(jnp.exp(steps), dims[axis_at] // shards_of).reshape((-1,) + (1,) * (len(dims) - 1 - axis_at))
    return loudness


def gaussian(own_key, shape, width, reach, split=(), dtype=jnp.bfloat16):
    drawn = width * jax.random.normal(own_key, shape, jnp.float32)
    if split:
        drawn = drawn * block_levels(own_key, shape, split, -0.22, 0.18)
    return jnp.clip(drawn, -reach, reach).astype(dtype)


def setup_inputs(seed: int = 0) -> dict:
    key_of = jax.random.split(jax.random.key(seed), 5)
    return {
        "image_field": gaussian(key_of[0], (CHANNELS, GRID, GRID), 1.0, 6.0, ((0, 4), (1, 8)), jnp.float32),
        "weights": jnp.clip(jnp.exp(math.log(1.0) - 2.9996462 * jax.random.uniform(key_of[1], (CHANNELS, GRID, GRID), jnp.float32) ** block_levels(key_of[1], (CHANNELS, GRID, GRID), ((0, 4), (2, 8)), -0.2, 0.2)), 0.049804688, 1.0).astype(jnp.bfloat16),
        "measured": gaussian(key_of[2], (CHANNELS, 2, GRID, GRID), 1.0, 6.0, ((0, 4), (3, 8))),
        "dual_field": gaussian(key_of[3], (CHANNELS, 2, GRID, GRID), 0.5, 3.0, ((2, 8), (3, 4))),
    }


step_primal = 0.5
step_dual = 0.5
clip_radius = 4.0

def reference(image_field, weights, measured, dual_field):

    def channel_gradient(inputs):
        channel_image, channel_weight, channel_data = inputs
        spectrum = jnp.fft.fft2(channel_image) / GRID
        residual = channel_weight.astype(jnp.float32) * spectrum - (channel_data[0].astype(jnp.float32) + 1j * channel_data[1].astype(jnp.float32))
        return jnp.real(jnp.fft.ifft2(residual)) * GRID
    gradient = lax.map(channel_gradient, (image_field, weights, measured))
    dual_rows = dual_field[:, 0].astype(jnp.float32)
    dual_cols = dual_field[:, 1].astype(jnp.float32)
    prev_rows = jnp.pad(dual_rows, ((0, 0), (1, 0), (0, 0)))[:, :-1, :]
    prev_cols = jnp.pad(dual_cols, ((0, 0), (0, 0), (1, 0)))[:, :, :-1]
    adjoint = prev_rows - dual_rows + prev_cols - dual_cols
    image_next = image_field - step_primal * (gradient + adjoint)
    extrapolated = 2.0 * image_next - image_field
    diff_rows = jnp.pad(extrapolated, ((0, 0), (0, 1), (0, 0)))[:, 1:, :] - extrapolated
    diff_cols = jnp.pad(extrapolated, ((0, 0), (0, 0), (0, 1)))[:, :, 1:] - extrapolated
    first_part = dual_rows + step_dual * diff_rows
    second_part = dual_cols + step_dual * diff_cols
    magnitude = jnp.sqrt(lax.optimization_barrier(jnp.sum(first_part * first_part + second_part * second_part, axis=0)))
    factor = 1.0 / jnp.maximum(1.0, magnitude / clip_radius)
    dual_next = jnp.stack([first_part * factor, second_part * factor], axis=1).astype(jnp.bfloat16)
    return (image_next, dual_next)
```

```python
from functools import partial
import math

import jax
import jax.numpy as jnp
import numpy as np
from jax import lax
from jax.experimental import pallas as pl
from jax.experimental.pallas import tpu as pltpu
from jax.sharding import PartitionSpec as P

step_primal = 0.5
step_dual = 0.5
clip_radius = 4.0
LANES = 128


def passed_along(x, axis, by):
    devices = lax.axis_size(axis)
    pairs = [(i, i + by) for i in range(devices) if 0 <= i + by < devices]
    return lax.ppermute(x, axis, pairs)


def turned(real, imag, num, den, sign):
    num = num % den
    if num == 0:
        return real, imag
    if 4 * num == den:
        return (-imag, real) if sign > 0 else (imag, -real)
    c = math.cos(2.0 * math.pi * num / den)
    s = sign * math.sin(2.0 * math.pi * num / den)
    if 8 * num == den:
        h = math.sqrt(0.5)
        if sign > 0:
            return (real - imag) * h, (real + imag) * h
        return (real + imag) * h, (imag - real) * h
    return real * c - imag * s, real * s + imag * c


def block_dft(values, sign):
    n = len(values)
    if n == 1:
        return values
    even = block_dft(values[0::2], sign)
    odd = block_dft(values[1::2], sign)
    low, high = [], []
    for k in range(n // 2):
        er, ei = even[k]
        tr, ti = turned(*odd[k], k, n, sign)
        low.append((er + tr, ei + ti))
        high.append((er - tr, ei - ti))
    return low + high


def halves(x):
    high = x.astype(jnp.bfloat16)
    return high, (x - high.astype(jnp.float32)).astype(jnp.bfloat16)


def exact_dot(first, second, dims):
    (fh, fl), (sh, sl) = first, second
    dot = partial(
        lax.dot_general, dimension_numbers=(dims, ((), ())), preferred_element_type=jnp.float32
    )
    return dot(fh, sh) + (dot(fh, sl) + dot(fl, sh))


def tables(blocks, inner):
    n = blocks * inner
    b = np.arange(blocks)[:, None, None]
    a = np.arange(inner)[None, :, None]
    i = np.arange(inner)[None, None, :]
    phase = 2.0 * np.pi / n * (((blocks * a + b) * i) % n)
    out = []
    for t in (np.cos(phase), np.sin(phase)):
        t = t.astype(np.float32)
        high = t.astype(jnp.bfloat16)
        low = (t - high.astype(np.float32)).astype(jnp.bfloat16)
        out += [high, low]
    return np.stack(out)


def kernel(
    F, CH, x_ref, t_ref, w_hbm, m_hbm, image_ref, grad_ref,
    xt, z, send, recv, wb, mb, wf, mf, u, sendy, recvy, gt, g,
    in_sem, fs, fr, bs, br, cs, cr, xs, xr, ls,
):
    R, N = x_ref.shape
    A = N // F
    C = A // LANES
    T = N // CH
    RC = R // LANES
    scale = 1.0 / N
    me = lax.axis_index("facet")
    mine = lax.axis_index("chan")
    order = sorted(range(1, F), key=lambda o: abs(o - F // 2))

    load_w = pltpu.make_async_copy(w_hbm.at[0], wb, in_sem.at[0])
    load_m = pltpu.make_async_copy(m_hbm.at[0], mb, in_sem.at[1])
    load_w.start()
    load_m.start()

    barrier = pltpu.get_barrier_semaphore()
    for o in range(1, F):
        pl.semaphore_signal(
            barrier, inc=1, device_id={"facet": lax.rem(me + o, F)},
            device_id_type=pl.DeviceIdType.MESH,
        )
    for o in range(1, CH):
        pl.semaphore_signal(
            barrier, inc=1, device_id={"chan": lax.rem(mine + o, CH)},
            device_id_type=pl.DeviceIdType.MESH,
        )
    pl.semaphore_wait(barrier, F - 1 + CH - 1)

    image_copies = []
    for o in range(1, CH):
        d = lax.rem(mine + o, CH)
        copy = pltpu.make_async_remote_copy(
            src_ref=x_ref.at[:, pl.ds(pl.multiple_of(d * T, LANES), T)],
            dst_ref=image_ref.at[mine],
            send_sem=xs.at[o], recv_sem=xr.at[o],
            device_id={"chan": d}, device_id_type=pl.DeviceIdType.MESH,
        )
        copy.start()
        image_copies.append(copy)
    own = pltpu.make_async_copy(
        x_ref.at[:, pl.ds(pl.multiple_of(mine * T, LANES), T)], image_ref.at[mine], ls.at[0]
    )
    own.start()
    image_copies.append(own)

    for i in range(RC):
        for j in range(N // LANES):
            xt[i, j * LANES:(j + 1) * LANES, :] = x_ref[
                i * LANES:(i + 1) * LANES, j * LANES:(j + 1) * LANES
            ].T

    @pl.loop(0, F)
    def _(b):
        lines = pl.ds(b, A, stride=F)
        part = halves(jnp.concatenate([xt[i, lines, :].T for i in range(RC)], axis=0))
        z[b, :, 0:A] = exact_dot(part, (t_ref[0, b], t_ref[1, b]), ((1,), (0,)))
        z[b, :, A:2 * A] = -exact_dot(part, (t_ref[2, b], t_ref[3, b]), ((1,), (0,)))

    copies = []
    for c in range(C):
        lo = c * LANES

        @pl.loop(0, R // 8)
        def _(t):
            rows = pl.ds(pl.multiple_of(t * 8, 8), 8)
            values = [
                (z[b, rows, lo:lo + LANES], z[b, rows, A + lo:A + lo + LANES]) for b in range(F)
            ]
            for j, (re, im) in enumerate(block_dft(values, -1.0)):
                send[c, j, rows, 0:LANES] = re
                send[c, j, rows, LANES:2 * LANES] = im

        group = []
        for o in order:
            d = lax.rem(me + o, F)
            copy = pltpu.make_async_remote_copy(
                src_ref=send.at[c, d], dst_ref=recv.at[c, me],
                send_sem=fs.at[c, o], recv_sem=fr.at[c, o],
                device_id={"facet": d}, device_id_type=pl.DeviceIdType.MESH,
            )
            copy.start()
            group.append(copy)
        copy = pltpu.make_async_copy(send.at[c, me], recv.at[c, me], fr.at[c, 0])
        copy.start()
        group.append(copy)
        copies.append(group)

    load_w.wait()
    load_m.wait()

    @pl.loop(0, N // 16)
    def _(t):
        rows = pl.ds(pl.multiple_of(t * 16, 16), 16)
        for c in range(C):
            lo = c * LANES
            wf[c, rows, :] = wb[rows, lo:lo + LANES].astype(jnp.float32) * scale
            mf[c, 0, rows, :] = mb[0, rows, lo:lo + LANES].astype(jnp.float32)
            mf[c, 1, rows, :] = mb[1, rows, lo:lo + LANES].astype(jnp.float32)

    for c in range(C):
        lo = c * LANES
        for copy in copies[c]:
            copy.wait()

        @pl.loop(0, R // 8)
        def _(t):
            rows = pl.ds(pl.multiple_of(t * 8, 8), 8)
            values = [
                (recv[c, q, rows, 0:LANES], recv[c, q, rows, LANES:2 * LANES]) for q in range(F)
            ]
            for k, (re, im) in enumerate(block_dft(values, -1.0)):
                u[k, rows, 0:LANES] = re
                u[k, rows, LANES:2 * LANES] = im

        @pl.loop(0, F)
        def _(k):
            cos, sin = (t_ref[0, k], t_ref[1, k]), (t_ref[2, k], t_ref[3, k])
            part = halves(u[k])
            p = exact_dot(cos, part, ((1,), (0,)))
            q = exact_dot(sin, part, ((1,), (0,)))
            spec_re = p[:, 0:LANES] + q[:, LANES:]
            spec_im = p[:, LANES:] - q[:, 0:LANES]
            lines = pl.ds(k, A, stride=F)
            weight = wf[c, lines, :]
            res_re = weight * spec_re - mf[c, 0, lines, :]
            res_im = weight * spec_im - mf[c, 1, lines, :]
            part = halves(jnp.concatenate([res_re, res_im], axis=1))
            p = exact_dot(cos, part, ((0,), (0,)))
            q = exact_dot(sin, part, ((0,), (0,)))
            u[k, :, 0:LANES] = p[:, 0:LANES] - q[:, LANES:]
            u[k, :, LANES:2 * LANES] = p[:, LANES:] + q[:, 0:LANES]

        @pl.loop(0, R // 8)
        def _(t):
            rows = pl.ds(pl.multiple_of(t * 8, 8), 8)
            values = [(u[k, rows, 0:LANES], u[k, rows, LANES:2 * LANES]) for k in range(F)]
            for q, (re, im) in enumerate(block_dft(values, 1.0)):
                sendy[q, rows, lo:lo + LANES] = re
                sendy[q, rows, A + lo:A + lo + LANES] = im

    back = []
    for h in range(RC):
        rows = pl.ds(h * LANES, LANES)
        group = []
        for o in order:
            d = lax.rem(me + o, F)
            copy = pltpu.make_async_remote_copy(
                src_ref=sendy.at[d, rows], dst_ref=recvy.at[me, rows],
                send_sem=bs.at[h, o], recv_sem=br.at[h, o],
                device_id={"facet": d}, device_id_type=pl.DeviceIdType.MESH,
            )
            copy.start()
            group.append(copy)
        copy = pltpu.make_async_copy(sendy.at[me, rows], recvy.at[me, rows], br.at[h, 0])
        copy.start()
        group.append(copy)
        back.append(group)

    last = []
    for h in range(RC):
        for copy in back[h]:
            copy.wait()

        @pl.loop(0, LANES // 8)
        def _(t):
            rows = pl.ds(pl.multiple_of(h * LANES + t * 8, 8), 8)
            for c in range(C):
                lo = c * LANES
                values = [
                    (recvy[j, rows, lo:lo + LANES], recvy[j, rows, A + lo:A + lo + LANES])
                    for j in range(F)
                ]
                for b, (re, im) in enumerate(block_dft(values, 1.0)):
                    z[b, rows, lo:lo + LANES] = re
                    z[b, rows, A + lo:A + lo + LANES] = im

        span = pl.ds(h * LANES, LANES)

        @pl.loop(0, F)
        def _(b):
            re, im = halves(z[b, span, 0:A]), halves(z[b, span, A:2 * A])
            line = exact_dot((t_ref[0, b], t_ref[1, b]), re, ((1,), (1,))) - exact_dot(
                (t_ref[2, b], t_ref[3, b]), im, ((1,), (1,))
            )
            gt[pl.ds(b, A, stride=F), :] = line * scale

        for j in range(N // LANES):
            g[span, j * LANES:(j + 1) * LANES] = gt[j * LANES:(j + 1) * LANES, :].T
        for o in range(1, CH):
            d = lax.rem(mine + o, CH)
            copy = pltpu.make_async_remote_copy(
                src_ref=g.at[span, pl.ds(pl.multiple_of(d * T, LANES), T)],
                dst_ref=grad_ref.at[mine, span],
                send_sem=cs.at[h, o], recv_sem=cr.at[h, o],
                device_id={"chan": d}, device_id_type=pl.DeviceIdType.MESH,
            )
            copy.start()
            last.append(copy)
        copy = pltpu.make_async_copy(
            g.at[span, pl.ds(pl.multiple_of(mine * T, LANES), T)],
            grad_ref.at[mine, span], ls.at[1 + h],
        )
        copy.start()
        last.append(copy)
    for copy in image_copies + last:
        copy.wait()


def gradient_tiles(F, CH, image, weights, measured):
    R, N = image.shape
    A = N // F
    C = A // LANES
    RC = R // LANES
    table = jnp.asarray(tables(F, A))
    tile = jax.ShapeDtypeStruct((CH, R, N // CH), jnp.float32)
    f32 = jnp.float32
    dma = pltpu.SemaphoreType.DMA
    vmem = pl.BlockSpec(memory_space=pltpu.VMEM)
    hbm = pl.BlockSpec(memory_space=pl.ANY)
    return pl.pallas_call(
        partial(kernel, F, CH),
        out_shape=(tile, tile),
        in_specs=[vmem, vmem, hbm, hbm],
        out_specs=(vmem, vmem),
        scratch_shapes=[
            pltpu.VMEM((RC, N, LANES), f32),
            pltpu.VMEM((F, R, 2 * A), f32),
            pltpu.VMEM((C, F, R, 2 * LANES), f32),
            pltpu.VMEM((C, F, R, 2 * LANES), f32),
            pltpu.VMEM((N, A), jnp.bfloat16),
            pltpu.VMEM((2, N, A), jnp.bfloat16),
            pltpu.VMEM((C, N, LANES), f32),
            pltpu.VMEM((C, 2, N, LANES), f32),
            pltpu.VMEM((F, A, 2 * LANES), f32),
            pltpu.VMEM((F, R, 2 * A), f32),
            pltpu.VMEM((F, R, 2 * A), f32),
            pltpu.VMEM((N, LANES), f32),
            pltpu.VMEM((R, N), f32),
            dma((2,)),
            dma((C, F)), dma((C, F)),
            dma((RC, F)), dma((RC, F)),
            dma((RC, CH)), dma((RC, CH)),
            dma((CH,)), dma((CH,)),
            dma((1 + RC,)),
        ],
        compiler_params=pltpu.CompilerParams(
            collective_id=0, has_side_effects=True, vmem_limit_bytes=60 * 1024 * 1024
        ),
    )(image, table, weights, measured)


def shards(image_field, weights, measured, dual_field):
    image_tile, gradient_tile = gradient_tiles(
        lax.axis_size("facet"), lax.axis_size("chan"), image_field[0], weights, measured
    )
    dual_rows = dual_field[:, 0].astype(jnp.float32)
    dual_cols = dual_field[:, 1].astype(jnp.float32)
    above = passed_along(dual_rows[:, -1:, :], "facet", 1)
    leftward = passed_along(dual_cols[:, :, -1], "chan", 1)
    prev_rows = jnp.concatenate([above, dual_rows[:, :-1, :]], axis=1)
    prev_cols = jnp.concatenate([leftward[:, :, None], dual_cols[:, :, :-1]], axis=2)
    adjoint = prev_rows - dual_rows + prev_cols - dual_cols
    image_next = image_tile - step_primal * (gradient_tile + adjoint)
    extrapolated = 2.0 * image_next - image_tile
    below = passed_along(extrapolated[:, :1, :], "facet", -1)
    rightward = passed_along(extrapolated[:, :, 0], "chan", -1)
    diff_rows = jnp.concatenate([extrapolated[:, 1:, :], below], axis=1) - extrapolated
    diff_cols = (
        jnp.concatenate([extrapolated[:, :, 1:], rightward[:, :, None]], axis=2) - extrapolated
    )
    first_part = dual_rows + step_dual * diff_rows
    second_part = dual_cols + step_dual * diff_cols
    magnitude = jnp.sqrt(jnp.sum(first_part * first_part + second_part * second_part, axis=0))
    factor = 1.0 / jnp.maximum(1.0, magnitude / clip_radius)
    dual_next = jnp.stack([first_part * factor, second_part * factor], axis=1).astype(jnp.bfloat16)
    return (image_next, dual_next)


def solution(mesh):
    placed = (
        P("chan", "facet", None),
        P("chan", None, "facet"),
        P("chan", None, None, "facet"),
        P(None, None, "facet", "chan"),
    )
    return jax.shard_map(
        shards,
        mesh=mesh,
        in_specs=placed,
        out_specs=(P(None, "facet", "chan"), P(None, None, "facet", "chan")),
        check_vma=False,
    )
```

```python
from functools import partial
import math

import jax
import jax.numpy as jnp
import numpy as np
from jax import lax
from jax.experimental import pallas as pl
from jax.experimental.pallas import tpu as pltpu
from jax.sharding import PartitionSpec as P

step_primal = 0.5
step_dual = 0.5
clip_radius = 4.0
LANES = 128


def passed_along(x, axis, by):
    devices = lax.axis_size(axis)
    pairs = [(i, i + by) for i in range(devices) if 0 <= i + by < devices]
    return lax.ppermute(x, axis, pairs)


def turned(real, imag, num, den, sign):
    num = num % den
    if num == 0:
        return real, imag
    if 4 * num == den:
        return (-imag, real) if sign > 0 else (imag, -real)
    c = math.cos(2.0 * math.pi * num / den)
    s = sign * math.sin(2.0 * math.pi * num / den)
    if 8 * num == den:
        h = math.sqrt(0.5)
        if sign > 0:
            return (real - imag) * h, (real + imag) * h
        return (real + imag) * h, (imag - real) * h
    return real * c - imag * s, real * s + imag * c


def block_dft(values, sign):
    n = len(values)
    if n == 1:
        return values
    even = block_dft(values[0::2], sign)
    odd = block_dft(values[1::2], sign)
    low, high = [], []
    for k in range(n // 2):
        er, ei = even[k]
        tr, ti = turned(*odd[k], k, n, sign)
        low.append((er + tr, ei + ti))
        high.append((er - tr, ei - ti))
    return low + high


def halves(x):
    high = x.astype(jnp.bfloat16)
    return high, (x - high.astype(jnp.float32)).astype(jnp.bfloat16)


def exact_dot(first, second, dims):
    (fh, fl), (sh, sl) = first, second
    dot = partial(
        lax.dot_general, dimension_numbers=(dims, ((), ())), preferred_element_type=jnp.float32
    )
    return dot(fh, sh) + (dot(fh, sl) + dot(fl, sh))


def tables(blocks, inner):
    n = blocks * inner
    b = np.arange(blocks)[:, None, None]
    a = np.arange(inner)[None, :, None]
    i = np.arange(inner)[None, None, :]
    phase = 2.0 * np.pi / n * (((blocks * a + b) * i) % n)
    pair = np.stack([np.cos(phase), -np.sin(phase)], axis=2).astype(np.float32)
    pair = pair.reshape(blocks, inner, 2, inner // LANES, LANES)
    pair = pair.transpose(0, 1, 3, 2, 4).reshape(blocks, inner, 2 * inner)
    high = pair.astype(jnp.bfloat16)
    low = (pair - high.astype(np.float32)).astype(jnp.bfloat16)
    return np.stack([high, low])


def square_tables(t_ref, k, chunks):
    found = []
    for at in (0, LANES):
        pieces = [
            [t_ref[s, k, :, 2 * LANES * c + at:2 * LANES * c + at + LANES] for c in range(chunks)]
            for s in (0, 1)
        ]
        found.append(tuple(jnp.concatenate(p, axis=1) if chunks > 1 else p[0] for p in pieces))
    return found


def kernel(
    F, CH, x_ref, t_ref, w_hbm, m_hbm, image_ref, grad_ref,
    xt, z, send, recv, wb, mb, wf, mf, u, sendy, recvy, gt, g,
    in_sem, fs, fr, bs, br, cs, cr, xs, xr, ls,
):
    R, N = x_ref.shape
    A = N // F
    C = A // LANES
    T = N // CH
    RC = R // LANES
    W = 2 * LANES
    scale = 1.0 / N
    me = lax.axis_index("facet")
    mine = lax.axis_index("chan")
    order = sorted(range(1, F), key=lambda o: abs(o - F // 2))

    load_w = pltpu.make_async_copy(w_hbm.at[0], wb, in_sem.at[0])
    load_m = pltpu.make_async_copy(m_hbm.at[0], mb, in_sem.at[1])
    load_w.start()
    load_m.start()

    barrier = pltpu.get_barrier_semaphore()
    for o in range(1, F):
        pl.semaphore_signal(
            barrier, inc=1, device_id={"facet": lax.rem(me + o, F)},
            device_id_type=pl.DeviceIdType.MESH,
        )
    for o in range(1, CH):
        pl.semaphore_signal(
            barrier, inc=1, device_id={"chan": lax.rem(mine + o, CH)},
            device_id_type=pl.DeviceIdType.MESH,
        )
    pl.semaphore_wait(barrier, F - 1 + CH - 1)

    image_copies = []
    for o in range(1, CH):
        d = lax.rem(mine + o, CH)
        copy = pltpu.make_async_remote_copy(
            src_ref=x_ref.at[:, pl.ds(pl.multiple_of(d * T, LANES), T)],
            dst_ref=image_ref.at[mine],
            send_sem=xs.at[o], recv_sem=xr.at[o],
            device_id={"chan": d}, device_id_type=pl.DeviceIdType.MESH,
        )
        copy.start()
        image_copies.append(copy)
    own = pltpu.make_async_copy(
        x_ref.at[:, pl.ds(pl.multiple_of(mine * T, LANES), T)], image_ref.at[mine], ls.at[0]
    )
    own.start()
    image_copies.append(own)

    copies = []
    for c in range(C):
        wide = slice(c * W, (c + 1) * W)
        group = []
        for h in range(RC):
            if c == 0:
                for j in range(N // LANES):
                    xt[h, j * LANES:(j + 1) * LANES, :] = x_ref[
                        h * LANES:(h + 1) * LANES, j * LANES:(j + 1) * LANES
                    ].T

            @pl.loop(0, F)
            def _(b):
                part = halves(xt[h, pl.ds(b, A, stride=F), :].T)
                table = (t_ref[0, b, :, wide], t_ref[1, b, :, wide])
                z[b, 0:LANES, 0:W] = exact_dot(part, table, ((1,), (0,)))

            @pl.loop(0, LANES // 8)
            def _(t):
                rows = pl.ds(pl.multiple_of(t * 8, 8), 8)
                target = pl.ds(pl.multiple_of(h * LANES + t * 8, 8), 8)
                values = [(z[b, rows, 0:LANES], z[b, rows, LANES:W]) for b in range(F)]
                for j, (re, im) in enumerate(block_dft(values, -1.0)):
                    send[c, j, target, 0:LANES] = re
                    send[c, j, target, LANES:W] = im

            span = pl.ds(h * LANES, LANES)
            for o in order:
                d = lax.rem(me + o, F)
                copy = pltpu.make_async_remote_copy(
                    src_ref=send.at[c, d, span], dst_ref=recv.at[c, me, span],
                    send_sem=fs.at[c, h, o], recv_sem=fr.at[c, h, o],
                    device_id={"facet": d}, device_id_type=pl.DeviceIdType.MESH,
                )
                copy.start()
                group.append(copy)
            copy = pltpu.make_async_copy(
                send.at[c, me, span], recv.at[c, me, span], fr.at[c, h, 0]
            )
            copy.start()
            group.append(copy)
        copies.append(group)

    load_w.wait()
    load_m.wait()

    @pl.loop(0, N // 16)
    def _(t):
        rows = pl.ds(pl.multiple_of(t * 16, 16), 16)
        for c in range(C):
            lo = c * LANES
            wf[c, rows, :] = wb[rows, lo:lo + LANES].astype(jnp.float32) * scale
            mf[c, 0, rows, :] = mb[0, rows, lo:lo + LANES].astype(jnp.float32)
            mf[c, 1, rows, :] = mb[1, rows, lo:lo + LANES].astype(jnp.float32)

    back = [[] for _ in range(RC)]
    for c in range(C):
        wide = slice(c * W, (c + 1) * W)
        for copy in copies[c]:
            copy.wait()

        @pl.loop(0, R // 8)
        def _(t):
            rows = pl.ds(pl.multiple_of(t * 8, 8), 8)
            values = [(recv[c, q, rows, 0:LANES], recv[c, q, rows, LANES:W]) for q in range(F)]
            for k, (re, im) in enumerate(block_dft(values, -1.0)):
                u[k, rows, 0:LANES] = re
                u[k, rows, LANES:W] = im

        @pl.loop(0, F)
        def _(k):
            cos, sin = square_tables(t_ref, k, C)
            part = halves(u[k])
            p = exact_dot(cos, part, ((1,), (0,)))
            q = exact_dot(sin, part, ((1,), (0,)))
            spec_re = p[:, 0:LANES] - q[:, LANES:]
            spec_im = p[:, LANES:] + q[:, 0:LANES]
            lines = pl.ds(k, A, stride=F)
            weight = wf[c, lines, :]
            res_re = weight * spec_re - mf[c, 0, lines, :]
            res_im = weight * spec_im - mf[c, 1, lines, :]
            part = halves(jnp.concatenate([res_re, res_im], axis=1))
            p = exact_dot(cos, part, ((0,), (0,)))
            q = exact_dot(sin, part, ((0,), (0,)))
            u[k, :, 0:LANES] = p[:, 0:LANES] + q[:, LANES:]
            u[k, :, LANES:W] = p[:, LANES:] - q[:, 0:LANES]

        for h in range(RC):

            @pl.loop(0, LANES // 8)
            def _(t):
                rows = pl.ds(pl.multiple_of(h * LANES + t * 8, 8), 8)
                values = [(u[k, rows, 0:LANES], u[k, rows, LANES:W]) for k in range(F)]
                for q, (re, im) in enumerate(block_dft(values, 1.0)):
                    sendy[q, rows, c * W:c * W + LANES] = re
                    sendy[q, rows, c * W + LANES:(c + 1) * W] = im

            span = pl.ds(h * LANES, LANES)
            for o in order:
                d = lax.rem(me + o, F)
                copy = pltpu.make_async_remote_copy(
                    src_ref=sendy.at[d, span, wide], dst_ref=recvy.at[me, span, wide],
                    send_sem=bs.at[c, h, o], recv_sem=br.at[c, h, o],
                    device_id={"facet": d}, device_id_type=pl.DeviceIdType.MESH,
                )
                copy.start()
                back[h].append(copy)
            copy = pltpu.make_async_copy(
                sendy.at[me, span, wide], recvy.at[me, span, wide], br.at[c, h, 0]
            )
            copy.start()
            back[h].append(copy)

    last = []
    for h in range(RC):
        for copy in back[h]:
            copy.wait()

        @pl.loop(0, LANES // 8)
        def _(t):
            rows = pl.ds(pl.multiple_of(h * LANES + t * 8, 8), 8)
            target = pl.ds(pl.multiple_of(t * 8, 8), 8)
            for c in range(C):
                re_at, im_at = pl.ds(c * W, LANES), pl.ds(c * W + LANES, LANES)
                values = [(recvy[j, rows, re_at], recvy[j, rows, im_at]) for j in range(F)]
                for b, (re, im) in enumerate(block_dft(values, 1.0)):
                    z[b, target, re_at] = re
                    z[b, target, im_at] = im

        span = pl.ds(h * LANES, LANES)

        @pl.loop(0, F)
        def _(b):
            line = exact_dot((t_ref[0, b], t_ref[1, b]), halves(z[b]), ((1,), (1,)))
            gt[pl.ds(b, A, stride=F), :] = line * scale

        for j in range(N // LANES):
            g[span, j * LANES:(j + 1) * LANES] = gt[j * LANES:(j + 1) * LANES, :].T
        for o in range(1, CH):
            d = lax.rem(mine + o, CH)
            copy = pltpu.make_async_remote_copy(
                src_ref=g.at[span, pl.ds(pl.multiple_of(d * T, LANES), T)],
                dst_ref=grad_ref.at[mine, span],
                send_sem=cs.at[h, o], recv_sem=cr.at[h, o],
                device_id={"chan": d}, device_id_type=pl.DeviceIdType.MESH,
            )
            copy.start()
            last.append(copy)
        copy = pltpu.make_async_copy(
            g.at[span, pl.ds(pl.multiple_of(mine * T, LANES), T)],
            grad_ref.at[mine, span], ls.at[1 + h],
        )
        copy.start()
        last.append(copy)
    for copy in image_copies + last:
        copy.wait()


def gradient_tiles(F, CH, image, weights, measured):
    R, N = image.shape
    A = N // F
    C = A // LANES
    RC = R // LANES
    table = jnp.asarray(tables(F, A))
    tile = jax.ShapeDtypeStruct((CH, R, N // CH), jnp.float32)
    f32 = jnp.float32
    dma = pltpu.SemaphoreType.DMA
    vmem = pl.BlockSpec(memory_space=pltpu.VMEM)
    hbm = pl.BlockSpec(memory_space=pl.ANY)
    return pl.pallas_call(
        partial(kernel, F, CH),
        out_shape=(tile, tile),
        in_specs=[vmem, vmem, hbm, hbm],
        out_specs=(vmem, vmem),
        scratch_shapes=[
            pltpu.VMEM((RC, N, LANES), f32),
            pltpu.VMEM((F, LANES, 2 * A), f32),
            pltpu.VMEM((C, F, R, 2 * LANES), f32),
            pltpu.VMEM((C, F, R, 2 * LANES), f32),
            pltpu.VMEM((N, A), jnp.bfloat16),
            pltpu.VMEM((2, N, A), jnp.bfloat16),
            pltpu.VMEM((C, N, LANES), f32),
            pltpu.VMEM((C, 2, N, LANES), f32),
            pltpu.VMEM((F, A, 2 * LANES), f32),
            pltpu.VMEM((F, R, 2 * A), f32),
            pltpu.VMEM((F, R, 2 * A), f32),
            pltpu.VMEM((N, LANES), f32),
            pltpu.VMEM((R, N), f32),
            dma((2,)),
            dma((C, RC, F)), dma((C, RC, F)),
            dma((C, RC, F)), dma((C, RC, F)),
            dma((RC, CH)), dma((RC, CH)),
            dma((CH,)), dma((CH,)),
            dma((1 + RC,)),
        ],
        compiler_params=pltpu.CompilerParams(
            collective_id=0, has_side_effects=True, vmem_limit_bytes=60 * 1024 * 1024
        ),
    )(image, table, weights, measured)


def shards(image_field, weights, measured, dual_field):
    image_tile, gradient_tile = gradient_tiles(
        lax.axis_size("facet"), lax.axis_size("chan"), image_field[0], weights, measured
    )
    dual_rows = dual_field[:, 0].astype(jnp.float32)
    dual_cols = dual_field[:, 1].astype(jnp.float32)
    above = passed_along(dual_rows[:, -1:, :], "facet", 1)
    leftward = passed_along(dual_cols[:, :, -1], "chan", 1)
    prev_rows = jnp.concatenate([above, dual_rows[:, :-1, :]], axis=1)
    prev_cols = jnp.concatenate([leftward[:, :, None], dual_cols[:, :, :-1]], axis=2)
    adjoint = prev_rows - dual_rows + prev_cols - dual_cols
    image_next = image_tile - step_primal * (gradient_tile + adjoint)
    extrapolated = 2.0 * image_next - image_tile
    below = passed_along(extrapolated[:, :1, :], "facet", -1)
    rightward = passed_along(extrapolated[:, :, 0], "chan", -1)
    diff_rows = jnp.concatenate([extrapolated[:, 1:, :], below], axis=1) - extrapolated
    diff_cols = (
        jnp.concatenate([extrapolated[:, :, 1:], rightward[:, :, None]], axis=2) - extrapolated
    )
    first_part = dual_rows + step_dual * diff_rows
    second_part = dual_cols + step_dual * diff_cols
    magnitude = jnp.sqrt(jnp.sum(first_part * first_part + second_part * second_part, axis=0))
    factor = 1.0 / jnp.maximum(1.0, magnitude / clip_radius)
    dual_next = jnp.stack([first_part * factor, second_part * factor], axis=1).astype(jnp.bfloat16)
    return (image_next, dual_next)


def solution(mesh):
    placed = (
        P("chan", "facet", None),
        P("chan", None, "facet"),
        P("chan", None, None, "facet"),
        P(None, None, "facet", "chan"),
    )
    return jax.shard_map(
        shards,
        mesh=mesh,
        in_specs=placed,
        out_specs=(P(None, "facet", "chan"), P(None, None, "facet", "chan")),
        check_vma=False,
    )
```

```python
from functools import partial
import math

import jax
import jax.numpy as jnp
import numpy as np
from jax import lax
from jax.experimental import pallas as pl
from jax.experimental.pallas import tpu as pltpu
from jax.sharding import PartitionSpec as P

step_primal = 0.5
step_dual = 0.5
clip_radius = 4.0
LANES = 128


def turned(real, imag, num, den, sign):
    num = num % den
    if num == 0:
        return real, imag
    if 4 * num == den:
        return (-imag, real) if sign > 0 else (imag, -real)
    c = math.cos(2.0 * math.pi * num / den)
    s = sign * math.sin(2.0 * math.pi * num / den)
    if 8 * num == den:
        h = math.sqrt(0.5)
        if sign > 0:
            return (real - imag) * h, (real + imag) * h
        return (real + imag) * h, (imag - real) * h
    return real * c - imag * s, real * s + imag * c


def block_dft(values, sign):
    n = len(values)
    if n == 1:
        return values
    even = block_dft(values[0::2], sign)
    odd = block_dft(values[1::2], sign)
    low, high = [], []
    for k in range(n // 2):
        er, ei = even[k]
        tr, ti = turned(*odd[k], k, n, sign)
        low.append((er + tr, ei + ti))
        high.append((er - tr, ei - ti))
    return low + high


def halves(x):
    high = x.astype(jnp.bfloat16)
    return high, (x - high.astype(jnp.float32)).astype(jnp.bfloat16)


def exact_dot(first, second, dims):
    (fh, fl), (sh, sl) = first, second
    dot = partial(
        lax.dot_general, dimension_numbers=(dims, ((), ())), preferred_element_type=jnp.float32
    )
    return dot(fh, sh) + (dot(fh, sl) + dot(fl, sh))


def tables(blocks, inner):
    n = blocks * inner
    b = np.arange(blocks)[:, None, None]
    a = np.arange(inner)[None, :, None]
    i = np.arange(inner)[None, None, :]
    phase = 2.0 * np.pi / n * (((blocks * a + b) * i) % n)
    pair = np.stack([np.cos(phase), -np.sin(phase)], axis=2).astype(np.float32)
    pair = pair.reshape(blocks, inner, 2, inner // LANES, LANES)
    pair = pair.transpose(0, 1, 3, 2, 4).reshape(blocks, inner, 2 * inner)
    high = pair.astype(jnp.bfloat16)
    low = (pair - high.astype(np.float32)).astype(jnp.bfloat16)
    return np.stack([high, low])


def square_tables(t_ref, k, chunks):
    found = []
    for at in (0, LANES):
        pieces = [
            [t_ref[s, k, :, 2 * LANES * c + at:2 * LANES * c + at + LANES] for c in range(chunks)]
            for s in (0, 1)
        ]
        found.append(tuple(jnp.concatenate(p, axis=1) if chunks > 1 else p[0] for p in pieces))
    return found


def halo_copy(source, target, send_sem, recv_sem, device):
    return pltpu.make_async_remote_copy(
        src_ref=source, dst_ref=target, send_sem=send_sem, recv_sem=recv_sem,
        device_id=device, device_id_type=pl.DeviceIdType.MESH,
    )


def kernel(
    F, CH, x_ref, t_ref, w_hbm, m_hbm, d_hbm,
    image_ref, grad_ref, up_ref, left_ref, low_ref, lowg_ref, right_ref, rightg_ref,
    dual, up, left, low, right,
    xt, z, send, recv, wb, mb, wf, mf, u, sendy, recvy, gt, g,
    in_sem, fs, fr, bs, br, cs, cr, xs, xr, ls, hs, hr, rs, rr, gs, gr,
):
    R, N = x_ref.shape
    A = N // F
    C = A // LANES
    T = N // CH
    RC = R // LANES
    W = 2 * LANES
    scale = 1.0 / N
    me = lax.axis_index("facet")
    mine = lax.axis_index("chan")
    order = sorted(range(1, F), key=lambda o: abs(o - F // 2))

    load_w = pltpu.make_async_copy(w_hbm.at[0], wb, in_sem.at[0])
    load_m = pltpu.make_async_copy(m_hbm.at[0], mb, in_sem.at[1])
    load_w.start()
    load_m.start()
    load_d = pltpu.make_async_copy(d_hbm, dual, in_sem.at[2])
    load_d.start()
    above, below = lax.rem(me + F - 1, F), lax.rem(me + 1, F)
    before, after = lax.rem(mine + CH - 1, CH), lax.rem(mine + 1, CH)

    barrier = pltpu.get_barrier_semaphore()
    for o in range(1, F):
        pl.semaphore_signal(
            barrier, inc=1, device_id={"facet": lax.rem(me + o, F)},
            device_id_type=pl.DeviceIdType.MESH,
        )
    for o in range(1, CH):
        pl.semaphore_signal(
            barrier, inc=1, device_id={"chan": lax.rem(mine + o, CH)},
            device_id_type=pl.DeviceIdType.MESH,
        )
        for f in (above, below):
            pl.semaphore_signal(
                barrier, inc=1, device_id={"chan": lax.rem(mine + o, CH), "facet": f},
                device_id_type=pl.DeviceIdType.MESH,
            )
    pl.semaphore_wait(barrier, F - 1 + 3 * (CH - 1))

    image_copies = []
    for o in range(1, CH):
        d = lax.rem(mine + o, CH)
        copy = pltpu.make_async_remote_copy(
            src_ref=x_ref.at[:, pl.ds(pl.multiple_of(d * T, LANES), T)],
            dst_ref=image_ref.at[mine],
            send_sem=xs.at[o], recv_sem=xr.at[o],
            device_id={"chan": d}, device_id_type=pl.DeviceIdType.MESH,
        )
        copy.start()
        image_copies.append(copy)
    own = pltpu.make_async_copy(
        x_ref.at[:, pl.ds(pl.multiple_of(mine * T, LANES), T)], image_ref.at[mine], ls.at[0]
    )
    own.start()
    image_copies.append(own)

    copies = []
    for c in range(C):
        wide = slice(c * W, (c + 1) * W)
        group = []
        for h in range(RC):
            if c == 0:
                for j in range(N // LANES):
                    xt[h, j * LANES:(j + 1) * LANES, :] = x_ref[
                        h * LANES:(h + 1) * LANES, j * LANES:(j + 1) * LANES
                    ].T

            @pl.loop(0, F)
            def _(b):
                part = halves(xt[h, pl.ds(b, A, stride=F), :].T)
                table = (t_ref[0, b, :, wide], t_ref[1, b, :, wide])
                z[b, 0:LANES, 0:W] = exact_dot(part, table, ((1,), (0,)))

            @pl.loop(0, LANES // 8)
            def _(t):
                rows = pl.ds(pl.multiple_of(t * 8, 8), 8)
                target = pl.ds(pl.multiple_of(h * LANES + t * 8, 8), 8)
                values = [(z[b, rows, 0:LANES], z[b, rows, LANES:W]) for b in range(F)]
                for j, (re, im) in enumerate(block_dft(values, -1.0)):
                    send[c, j, target, 0:LANES] = re
                    send[c, j, target, LANES:W] = im

            span = pl.ds(h * LANES, LANES)
            for o in order:
                d = lax.rem(me + o, F)
                copy = pltpu.make_async_remote_copy(
                    src_ref=send.at[c, d, span], dst_ref=recv.at[c, me, span],
                    send_sem=fs.at[c, h, o], recv_sem=fr.at[c, h, o],
                    device_id={"facet": d}, device_id_type=pl.DeviceIdType.MESH,
                )
                copy.start()
                group.append(copy)
            copy = pltpu.make_async_copy(
                send.at[c, me, span], recv.at[c, me, span], fr.at[c, h, 0]
            )
            copy.start()
            group.append(copy)
        copies.append(group)

    load_d.wait()
    for k in range(CH):
        up[k] = dual[k, 0, R - 16:R, :].astype(jnp.float32)[8:16, :]
        left[k] = dual[k, 1, :, T - LANES:T].astype(jnp.float32)
    halos = [
        halo_copy(up, up_ref, hs.at[0], hr.at[0], {"facet": below}),
        halo_copy(left, left_ref, hs.at[1], hr.at[1], {"chan": after}),
    ]
    for copy in halos:
        copy.start()
    for copy in image_copies + halos:
        copy.wait()
    for k in range(CH):
        first_up = jnp.where(me > 0, up_ref[k], 0.0)[7:8, :]
        first_left = jnp.where(mine > 0, left_ref[k], 0.0)[:, LANES - 1:LANES]
        p = dual[k, 0, 0:16, :].astype(jnp.float32)[0:8, :]
        q = dual[k, 1, 0:16, :].astype(jnp.float32)[0:8, :]
        lane = lax.broadcasted_iota(jnp.int32, (8, T), 1)
        q_prev = jnp.where(lane == 0, first_left[0:8, :], pltpu.roll(q, 1, 1))
        low[k] = image_ref[k, 0:8, :] - (first_up - p + q_prev - q)
        p = dual[k, 0, :, 0:LANES].astype(jnp.float32)
        q = dual[k, 1, :, 0:LANES].astype(jnp.float32)
        row = lax.broadcasted_iota(jnp.int32, (R, LANES), 0)
        p_prev = jnp.where(row == 0, first_up[:, 0:LANES], pltpu.roll(p, 1, 0))
        right[k] = image_ref[k, :, 0:LANES] - (p_prev - p + first_left - q)
    edges = [
        halo_copy(low, low_ref, hs.at[2], hr.at[2], {"facet": above}),
        halo_copy(right, right_ref, hs.at[3], hr.at[3], {"chan": before}),
    ]
    for copy in edges:
        copy.start()

    load_w.wait()
    load_m.wait()

    @pl.loop(0, N // 16)
    def _(t):
        rows = pl.ds(pl.multiple_of(t * 16, 16), 16)
        for c in range(C):
            lo = c * LANES
            wf[c, rows, :] = wb[rows, lo:lo + LANES].astype(jnp.float32) * scale
            mf[c, 0, rows, :] = mb[0, rows, lo:lo + LANES].astype(jnp.float32)
            mf[c, 1, rows, :] = mb[1, rows, lo:lo + LANES].astype(jnp.float32)

    back = [[] for _ in range(RC)]
    for c in range(C):
        wide = slice(c * W, (c + 1) * W)
        for copy in copies[c]:
            copy.wait()

        @pl.loop(0, R // 8)
        def _(t):
            rows = pl.ds(pl.multiple_of(t * 8, 8), 8)
            values = [(recv[c, q, rows, 0:LANES], recv[c, q, rows, LANES:W]) for q in range(F)]
            for k, (re, im) in enumerate(block_dft(values, -1.0)):
                u[k, rows, 0:LANES] = re
                u[k, rows, LANES:W] = im

        @pl.loop(0, F)
        def _(k):
            cos, sin = square_tables(t_ref, k, C)
            part = halves(u[k])
            p = exact_dot(cos, part, ((1,), (0,)))
            q = exact_dot(sin, part, ((1,), (0,)))
            spec_re = p[:, 0:LANES] - q[:, LANES:]
            spec_im = p[:, LANES:] + q[:, 0:LANES]
            lines = pl.ds(k, A, stride=F)
            weight = wf[c, lines, :]
            res_re = weight * spec_re - mf[c, 0, lines, :]
            res_im = weight * spec_im - mf[c, 1, lines, :]
            part = halves(jnp.concatenate([res_re, res_im], axis=1))
            p = exact_dot(cos, part, ((0,), (0,)))
            q = exact_dot(sin, part, ((0,), (0,)))
            u[k, :, 0:LANES] = p[:, 0:LANES] + q[:, LANES:]
            u[k, :, LANES:W] = p[:, LANES:] - q[:, 0:LANES]

        for h in range(RC):

            @pl.loop(0, LANES // 8)
            def _(t):
                rows = pl.ds(pl.multiple_of(h * LANES + t * 8, 8), 8)
                values = [(u[k, rows, 0:LANES], u[k, rows, LANES:W]) for k in range(F)]
                for q, (re, im) in enumerate(block_dft(values, 1.0)):
                    sendy[q, rows, c * W:c * W + LANES] = re
                    sendy[q, rows, c * W + LANES:(c + 1) * W] = im

            span = pl.ds(h * LANES, LANES)
            for o in order:
                d = lax.rem(me + o, F)
                copy = pltpu.make_async_remote_copy(
                    src_ref=sendy.at[d, span, wide], dst_ref=recvy.at[me, span, wide],
                    send_sem=bs.at[c, h, o], recv_sem=br.at[c, h, o],
                    device_id={"facet": d}, device_id_type=pl.DeviceIdType.MESH,
                )
                copy.start()
                back[h].append(copy)
            copy = pltpu.make_async_copy(
                sendy.at[me, span, wide], recvy.at[me, span, wide], br.at[c, h, 0]
            )
            copy.start()
            back[h].append(copy)

    last = []
    for h in range(RC):
        for copy in back[h]:
            copy.wait()

        @pl.loop(0, LANES // 8)
        def _(t):
            rows = pl.ds(pl.multiple_of(h * LANES + t * 8, 8), 8)
            target = pl.ds(pl.multiple_of(t * 8, 8), 8)
            for c in range(C):
                re_at, im_at = pl.ds(c * W, LANES), pl.ds(c * W + LANES, LANES)
                values = [(recvy[j, rows, re_at], recvy[j, rows, im_at]) for j in range(F)]
                for b, (re, im) in enumerate(block_dft(values, 1.0)):
                    z[b, target, re_at] = re
                    z[b, target, im_at] = im

        span = pl.ds(h * LANES, LANES)

        @pl.loop(0, F)
        def _(b):
            line = exact_dot((t_ref[0, b], t_ref[1, b]), halves(z[b]), ((1,), (1,)))
            gt[pl.ds(b, A, stride=F), :] = line * scale

        for j in range(N // LANES):
            g[span, j * LANES:(j + 1) * LANES] = gt[j * LANES:(j + 1) * LANES, :].T
        if h == 0:
            for o in range(CH):
                d = lax.rem(mine + o, CH)
                copy = halo_copy(
                    g.at[0:8, pl.ds(pl.multiple_of(d * T, LANES), T)], lowg_ref.at[mine],
                    gs.at[o], gr.at[o], {"chan": d, "facet": above},
                )
                copy.start()
                last.append(copy)
        for o in range(1, CH):
            d = lax.rem(mine + o, CH)
            e = lax.rem(mine + o + 1, CH)
            copy = halo_copy(
                g.at[span, pl.ds(pl.multiple_of(e * T, LANES), LANES)],
                rightg_ref.at[mine, span], rs.at[h, o], rr.at[h, o], {"chan": d},
            )
            copy.start()
            last.append(copy)
            copy = pltpu.make_async_remote_copy(
                src_ref=g.at[span, pl.ds(pl.multiple_of(d * T, LANES), T)],
                dst_ref=grad_ref.at[mine, span],
                send_sem=cs.at[h, o], recv_sem=cr.at[h, o],
                device_id={"chan": d}, device_id_type=pl.DeviceIdType.MESH,
            )
            copy.start()
            last.append(copy)
        copy = pltpu.make_async_copy(
            g.at[span, pl.ds(pl.multiple_of(mine * T, LANES), T)],
            grad_ref.at[mine, span], ls.at[1 + h],
        )
        copy.start()
        last.append(copy)
        copy = pltpu.make_async_copy(
            g.at[span, pl.ds(pl.multiple_of(after * T, LANES), LANES)],
            rightg_ref.at[mine, span], rr.at[h, 0],
        )
        copy.start()
        last.append(copy)
    for copy in edges + last:
        copy.wait()


def gradient_tiles(F, CH, image, weights, measured, dual):
    R, N = image.shape
    A = N // F
    C = A // LANES
    RC = R // LANES
    table = jnp.asarray(tables(F, A))
    T = N // CH
    tile = jax.ShapeDtypeStruct((CH, R, T), jnp.float32)
    line = jax.ShapeDtypeStruct((CH, 8, T), jnp.float32)
    side = jax.ShapeDtypeStruct((CH, R, LANES), jnp.float32)
    f32 = jnp.float32
    dma = pltpu.SemaphoreType.DMA
    vmem = pl.BlockSpec(memory_space=pltpu.VMEM)
    hbm = pl.BlockSpec(memory_space=pl.ANY)
    return pl.pallas_call(
        partial(kernel, F, CH),
        out_shape=(tile, tile, line, side, line, line, side, side),
        in_specs=[vmem, vmem, hbm, hbm, hbm],
        out_specs=(vmem,) * 8,
        scratch_shapes=[
            pltpu.VMEM((CH, 2, R, T), jnp.bfloat16),
            pltpu.VMEM((CH, 8, T), f32),
            pltpu.VMEM((CH, R, LANES), f32),
            pltpu.VMEM((CH, 8, T), f32),
            pltpu.VMEM((CH, R, LANES), f32),
            pltpu.VMEM((RC, N, LANES), f32),
            pltpu.VMEM((F, LANES, 2 * A), f32),
            pltpu.VMEM((C, F, R, 2 * LANES), f32),
            pltpu.VMEM((C, F, R, 2 * LANES), f32),
            pltpu.VMEM((N, A), jnp.bfloat16),
            pltpu.VMEM((2, N, A), jnp.bfloat16),
            pltpu.VMEM((C, N, LANES), f32),
            pltpu.VMEM((C, 2, N, LANES), f32),
            pltpu.VMEM((F, A, 2 * LANES), f32),
            pltpu.VMEM((F, R, 2 * A), f32),
            pltpu.VMEM((F, R, 2 * A), f32),
            pltpu.VMEM((N, LANES), f32),
            pltpu.VMEM((R, N), f32),
            dma((3,)),
            dma((C, RC, F)), dma((C, RC, F)),
            dma((C, RC, F)), dma((C, RC, F)),
            dma((RC, CH)), dma((RC, CH)),
            dma((CH,)), dma((CH,)),
            dma((1 + RC,)),
            dma((4,)), dma((4,)),
            dma((RC, CH)), dma((RC, CH)),
            dma((CH,)), dma((CH,)),
        ],
        compiler_params=pltpu.CompilerParams(
            collective_id=0, has_side_effects=True, vmem_limit_bytes=60 * 1024 * 1024
        ),
    )(image, table, weights, measured, dual)


def prior_kernel(
    n, edge, x, g, d, up, left, low, lowg, right, rightg, image, dual, ext, held, carry, parts
):
    t = pl.program_id(0)
    CH, TR, T = x.shape
    now = lax.rem(t, 2)
    row = lax.broadcasted_iota(jnp.int32, (TR, T), 0)
    lane = lax.broadcasted_iota(jnp.int32, (TR, T), 1)

    @pl.when(t == 0)
    def _():
        carry[...] = jnp.where(edge[0] == 0, 0.0, up[...])

    @pl.when(t < n)
    def _():
        for c in range(CH):
            p = d[c, 0].astype(jnp.float32)
            q = d[c, 1].astype(jnp.float32)
            p_prev = jnp.where(row == 0, carry[c, 7:8, :], pltpu.roll(p, 1, 0))
            first = jnp.where(edge[2] == 0, 0.0, left[c])[:, LANES - 1:LANES]
            q_prev = jnp.where(lane == 0, first, pltpu.roll(q, 1, 1))
            adjoint = p_prev - p + q_prev - q
            value = x[c] - step_primal * (g[c] + adjoint)
            image[c] = value
            ext[now, c] = 2.0 * value - x[c]
            held[now, c, 0] = p
            held[now, c, 1] = q
            carry[c] = p[TR - 8:TR, :]

    @pl.when(t > 0)
    def _():
        was = 1 - now
        total = jnp.zeros((TR, T), jnp.float32)
        for c in range(CH):
            e = ext[was, c]
            beyond = jnp.where(edge[1] == 0, 0.0, low[c] - lowg[c])
            following = jnp.where(t < n, ext[now, c, 0:8, :], beyond)[0:1, :]
            rows = jnp.where(row == TR - 1, following, pltpu.roll(e, TR - 1, 0)) - e
            side = jnp.where(edge[3] == 0, 0.0, right[c] - rightg[c])[:, 0:1]
            cols = jnp.where(lane == T - 1, side, pltpu.roll(e, T - 1, 1)) - e
            first_part = held[was, c, 0] + step_dual * rows
            second_part = held[was, c, 1] + step_dual * cols
            parts[c, 0] = first_part
            parts[c, 1] = second_part
            total = total + (first_part * first_part + second_part * second_part)
        factor = 1.0 / jnp.maximum(1.0, jnp.sqrt(total) / clip_radius)
        for c in range(CH):
            dual[c, 0] = (parts[c, 0] * factor).astype(jnp.bfloat16)
            dual[c, 1] = (parts[c, 1] * factor).astype(jnp.bfloat16)


def prior(edge, x, g, dual, up, left, low, lowg, right, rightg):
    CH, R, T = x.shape
    TR = 32
    n = R // TR
    f32 = jnp.float32
    ahead = lambda t: jnp.minimum(t, n - 1)
    behind = lambda t: jnp.maximum(t - 1, 0)
    tile = pl.BlockSpec((CH, TR, T), lambda t: (0, ahead(t), 0))
    line = pl.BlockSpec((CH, 8, T), lambda t: (0, 0, 0))
    return pl.pallas_call(
        partial(prior_kernel, n),
        grid=(n + 1,),
        out_shape=(
            jax.ShapeDtypeStruct((CH, R, T), f32),
            jax.ShapeDtypeStruct((CH, 2, R, T), jnp.bfloat16),
        ),
        in_specs=[
            pl.BlockSpec(memory_space=pltpu.SMEM),
            tile,
            tile,
            pl.BlockSpec((CH, 2, TR, T), lambda t: (0, 0, ahead(t), 0)),
            line,
            pl.BlockSpec((CH, TR, LANES), lambda t: (0, ahead(t), 0)),
            line,
            line,
            pl.BlockSpec((CH, TR, LANES), lambda t: (0, behind(t), 0)),
            pl.BlockSpec((CH, TR, LANES), lambda t: (0, behind(t), 0)),
        ],
        out_specs=(tile, pl.BlockSpec((CH, 2, TR, T), lambda t: (0, 0, behind(t), 0))),
        scratch_shapes=[
            pltpu.VMEM((2, CH, TR, T), f32),
            pltpu.VMEM((2, CH, 2, TR, T), f32),
            pltpu.VMEM((CH, 8, T), f32),
            pltpu.VMEM((CH, 2, TR, T), f32),
        ],
        compiler_params=pltpu.CompilerParams(vmem_limit_bytes=24 * 1024 * 1024),
    )(edge, x, g, dual, up, left, low, lowg, right, rightg)


def shards(image_field, weights, measured, dual_field):
    F, CH = lax.axis_size("facet"), lax.axis_size("chan")
    tiles = gradient_tiles(F, CH, image_field[0], weights, measured, dual_field)
    f, c = lax.axis_index("facet"), lax.axis_index("chan")
    edge = jnp.stack([f > 0, f < F - 1, c > 0, c < CH - 1]).astype(jnp.int32)
    return prior(edge, tiles[0], tiles[1], dual_field, *tiles[2:])


def solution(mesh):
    placed = (
        P("chan", "facet", None),
        P("chan", None, "facet"),
        P("chan", None, None, "facet"),
        P(None, None, "facet", "chan"),
    )
    return jax.shard_map(
        shards,
        mesh=mesh,
        in_specs=placed,
        out_specs=(P(None, "facet", "chan"), P(None, None, "facet", "chan")),
        check_vma=False,
    )
```

```python
from functools import partial
import math

import jax
import jax.numpy as jnp
import numpy as np
from jax import lax
from jax.experimental import pallas as pl
from jax.experimental.pallas import tpu as pltpu
from jax.sharding import PartitionSpec as P

step_primal = 0.5
step_dual = 0.5
clip_radius = 4.0
LANES = 128


def turned(real, imag, num, den, sign):
    num = num % den
    if num == 0:
        return real, imag
    if 4 * num == den:
        return (-imag, real) if sign > 0 else (imag, -real)
    c = math.cos(2.0 * math.pi * num / den)
    s = sign * math.sin(2.0 * math.pi * num / den)
    if 8 * num == den:
        h = math.sqrt(0.5)
        if sign > 0:
            return (real - imag) * h, (real + imag) * h
        return (real + imag) * h, (imag - real) * h
    return real * c - imag * s, real * s + imag * c


def block_dft(values, sign):
    n = len(values)
    if n == 1:
        return values
    even = block_dft(values[0::2], sign)
    odd = block_dft(values[1::2], sign)
    low, high = [], []
    for k in range(n // 2):
        er, ei = even[k]
        tr, ti = turned(*odd[k], k, n, sign)
        low.append((er + tr, ei + ti))
        high.append((er - tr, ei - ti))
    return low + high


def halves(x):
    high = x.astype(jnp.bfloat16)
    return high, (x - high.astype(jnp.float32)).astype(jnp.bfloat16)


def exact_dot(first, second, dims):
    (fh, fl), (sh, sl) = first, second
    dot = partial(
        lax.dot_general, dimension_numbers=(dims, ((), ())), preferred_element_type=jnp.float32
    )
    return dot(fh, sh) + (dot(fh, sl) + dot(fl, sh))


def table_seeds(blocks, inner):
    n = blocks * inner
    a = np.arange(max(blocks, inner))[:, None]
    i = np.arange(inner)[None, :]

    def pairs(step, count):
        phase = 2.0 * np.pi / n * ((step * a[:count] * i) % n)
        pair = np.stack([np.cos(phase), -np.sin(phase)], axis=1).astype(np.float32)
        pair = pair.reshape(count, 2, inner // LANES, LANES)
        return pair.transpose(0, 2, 1, 3).reshape(count, 2 * inner)

    return pairs(blocks, inner), np.repeat(pairs(1, blocks)[:, None, :], 8, axis=1)


def fill_tables(seed_ref, turn_ref, t_ref):
    _, F, A, width = t_ref.shape

    @pl.loop(0, F)
    def _(b):
        for c in range(width // (2 * LANES)):
            re_at = slice(2 * c * LANES, (2 * c + 1) * LANES)
            im_at = slice((2 * c + 1) * LANES, (2 * c + 2) * LANES)
            turn_re, turn_im = turn_ref[b, 0:1, re_at], turn_ref[b, 0:1, im_at]

            @pl.loop(0, A // 32)
            def _(t):
                rows = pl.ds(pl.multiple_of(t * 32, 32), 32)
                re, im = seed_ref[rows, re_at], seed_ref[rows, im_at]
                pair = (re * turn_re - im * turn_im, re * turn_im + im * turn_re)
                for value, at in zip(pair, (re_at, im_at)):
                    high, low = halves(value)
                    t_ref[0, b, rows, at] = high
                    t_ref[1, b, rows, at] = low


def back_pieces(rows):
    pieces, start = [], 0
    while rows - start > 32:
        size = min(LANES, (rows - start) // 2)
        pieces.append((start, size))
        start += size
    return pieces + [(start, rows - start)]


def square_tables(t_ref, k, chunks):
    found = []
    for at in (0, LANES):
        pieces = [
            [t_ref[s, k, :, 2 * LANES * c + at:2 * LANES * c + at + LANES] for c in range(chunks)]
            for s in (0, 1)
        ]
        found.append(tuple(jnp.concatenate(p, axis=1) if chunks > 1 else p[0] for p in pieces))
    return found


def halo_copy(source, target, send_sem, recv_sem, device):
    return pltpu.make_async_remote_copy(
        src_ref=source, dst_ref=target, send_sem=send_sem, recv_sem=recv_sem,
        device_id=device, device_id_type=pl.DeviceIdType.MESH,
    )


def kernel(
    F, CH, x_ref, seed_ref, turn_ref, w_hbm, m_hbm, d_hbm,
    image_hbm, grad_ref, up_hbm, left_hbm, low_ref, lowg_ref, right_ref, rightg_ref,
    t_ref, image_ref, up_ref, left_ref, dual, up, left, low, right,
    xt, z, send, recv, wb, mb, wf, mf, u, sendy, recvy, gt, g,
    in_sem, fs, fr, bs, br, cs, cr, xs, xr, ls, hs, hr, rs, rr, gs, gr,
):
    R, N = x_ref.shape
    A = N // F
    C = A // LANES
    T = N // CH
    RC = R // LANES
    W = 2 * LANES
    scale = 1.0 / N
    me = lax.axis_index("facet")
    mine = lax.axis_index("chan")
    order = sorted(range(1, F), key=lambda o: abs(o - F // 2))

    load_w = pltpu.make_async_copy(w_hbm.at[0], wb, in_sem.at[0])
    load_m = pltpu.make_async_copy(m_hbm.at[0], mb, in_sem.at[1])
    load_w.start()
    load_m.start()
    load_d = pltpu.make_async_copy(d_hbm, dual, in_sem.at[2])
    load_d.start()
    above, below = lax.rem(me + F - 1, F), lax.rem(me + 1, F)
    before, after = lax.rem(mine + CH - 1, CH), lax.rem(mine + 1, CH)

    barrier = pltpu.get_barrier_semaphore()
    for o in range(1, F):
        pl.semaphore_signal(
            barrier, inc=1, device_id={"facet": lax.rem(me + o, F)},
            device_id_type=pl.DeviceIdType.MESH,
        )
    for o in range(1, CH):
        pl.semaphore_signal(
            barrier, inc=1, device_id={"chan": lax.rem(mine + o, CH)},
            device_id_type=pl.DeviceIdType.MESH,
        )
        for f in (above, below):
            pl.semaphore_signal(
                barrier, inc=1, device_id={"chan": lax.rem(mine + o, CH), "facet": f},
                device_id_type=pl.DeviceIdType.MESH,
            )
    fill_tables(seed_ref, turn_ref, t_ref)
    pl.semaphore_wait(barrier, F - 1 + 3 * (CH - 1))

    image_copies = []
    for o in range(1, CH):
        d = lax.rem(mine + o, CH)
        copy = pltpu.make_async_remote_copy(
            src_ref=x_ref.at[:, pl.ds(pl.multiple_of(d * T, LANES), T)],
            dst_ref=image_ref.at[mine],
            send_sem=xs.at[o], recv_sem=xr.at[o],
            device_id={"chan": d}, device_id_type=pl.DeviceIdType.MESH,
        )
        copy.start()
        image_copies.append(copy)
    own = pltpu.make_async_copy(
        x_ref.at[:, pl.ds(pl.multiple_of(mine * T, LANES), T)], image_ref.at[mine], ls.at[0]
    )
    own.start()
    image_copies.append(own)

    copies = []
    for c in range(C):
        wide = slice(c * W, (c + 1) * W)
        group = []
        for h in range(RC):
            if c == 0:
                for j in range(N // LANES):
                    xt[h, j * LANES:(j + 1) * LANES, :] = x_ref[
                        h * LANES:(h + 1) * LANES, j * LANES:(j + 1) * LANES
                    ].T

            @pl.loop(0, F)
            def _(b):
                part = halves(xt[h, pl.ds(b, A, stride=F), :].T)
                table = (t_ref[0, b, :, wide], t_ref[1, b, :, wide])
                z[b, 0:LANES, 0:W] = exact_dot(part, table, ((1,), (0,)))

            @pl.loop(0, LANES // 8)
            def _(t):
                rows = pl.ds(pl.multiple_of(t * 8, 8), 8)
                target = pl.ds(pl.multiple_of(h * LANES + t * 8, 8), 8)
                values = [(z[b, rows, 0:LANES], z[b, rows, LANES:W]) for b in range(F)]
                for j, (re, im) in enumerate(block_dft(values, -1.0)):
                    send[c, j, target, 0:LANES] = re
                    send[c, j, target, LANES:W] = im

            span = pl.ds(h * LANES, LANES)
            for o in order:
                d = lax.rem(me + o, F)
                copy = pltpu.make_async_remote_copy(
                    src_ref=send.at[c, d, span], dst_ref=recv.at[c, me, span],
                    send_sem=fs.at[c, h, o], recv_sem=fr.at[c, h, o],
                    device_id={"facet": d}, device_id_type=pl.DeviceIdType.MESH,
                )
                copy.start()
                group.append(copy)
            copy = pltpu.make_async_copy(
                send.at[c, me, span], recv.at[c, me, span], fr.at[c, h, 0]
            )
            copy.start()
            group.append(copy)
        copies.append(group)

    load_d.wait()
    for k in range(CH):
        up[k] = dual[k, 0, R - 16:R, :].astype(jnp.float32)[8:16, :]
        left[k] = dual[k, 1, :, T - LANES:T].astype(jnp.float32)
    halos = [
        halo_copy(up, up_ref, hs.at[0], hr.at[0], {"facet": below}),
        halo_copy(left, left_ref, hs.at[1], hr.at[1], {"chan": after}),
    ]
    for copy in halos:
        copy.start()
    for copy in image_copies + halos:
        copy.wait()
    edges = [
        pltpu.make_async_copy(image_ref, image_hbm, in_sem.at[3]),
        pltpu.make_async_copy(up_ref, up_hbm, in_sem.at[4]),
        pltpu.make_async_copy(left_ref, left_hbm, in_sem.at[5]),
    ]
    for k in range(CH):
        first_up = jnp.where(me > 0, up_ref[k], 0.0)[7:8, :]
        first_left = jnp.where(mine > 0, left_ref[k], 0.0)[:, LANES - 1:LANES]
        p = dual[k, 0, 0:16, :].astype(jnp.float32)[0:8, :]
        q = dual[k, 1, 0:16, :].astype(jnp.float32)[0:8, :]
        lane = lax.broadcasted_iota(jnp.int32, (8, T), 1)
        q_prev = jnp.where(lane == 0, first_left[0:8, :], pltpu.roll(q, 1, 1))
        low[k] = image_ref[k, 0:8, :] - (first_up - p + q_prev - q)
        p = dual[k, 0, :, 0:LANES].astype(jnp.float32)
        q = dual[k, 1, :, 0:LANES].astype(jnp.float32)
        row = lax.broadcasted_iota(jnp.int32, (R, LANES), 0)
        p_prev = jnp.where(row == 0, first_up[:, 0:LANES], pltpu.roll(p, 1, 0))
        right[k] = image_ref[k, :, 0:LANES] - (p_prev - p + first_left - q)
    edges += [
        halo_copy(low, low_ref, hs.at[2], hr.at[2], {"facet": above}),
        halo_copy(right, right_ref, hs.at[3], hr.at[3], {"chan": before}),
    ]
    for copy in edges:
        copy.start()

    load_w.wait()
    load_m.wait()

    @pl.loop(0, N // 16)
    def _(t):
        rows = pl.ds(pl.multiple_of(t * 16, 16), 16)
        for c in range(C):
            lo = c * LANES
            wf[c, rows, :] = wb[rows, lo:lo + LANES].astype(jnp.float32) * scale
            mf[c, 0, rows, :] = mb[0, rows, lo:lo + LANES].astype(jnp.float32)
            mf[c, 1, rows, :] = mb[1, rows, lo:lo + LANES].astype(jnp.float32)

    pieces = back_pieces(R)
    back = [[] for _ in pieces]
    for c in range(C):
        wide = slice(c * W, (c + 1) * W)
        for copy in copies[c]:
            copy.wait()

        @pl.loop(0, R // 8)
        def _(t):
            rows = pl.ds(pl.multiple_of(t * 8, 8), 8)
            values = [(recv[c, q, rows, 0:LANES], recv[c, q, rows, LANES:W]) for q in range(F)]
            for k, (re, im) in enumerate(block_dft(values, -1.0)):
                u[k, rows, 0:LANES] = re
                u[k, rows, LANES:W] = im

        @pl.loop(0, F)
        def _(k):
            cos, sin = square_tables(t_ref, k, C)
            part = halves(u[k])
            p = exact_dot(cos, part, ((1,), (0,)))
            q = exact_dot(sin, part, ((1,), (0,)))
            spec_re = p[:, 0:LANES] - q[:, LANES:]
            spec_im = p[:, LANES:] + q[:, 0:LANES]
            lines = pl.ds(k, A, stride=F)
            weight = wf[c, lines, :]
            res_re = weight * spec_re - mf[c, 0, lines, :]
            res_im = weight * spec_im - mf[c, 1, lines, :]
            part = halves(jnp.concatenate([res_re, res_im], axis=1))
            p = exact_dot(cos, part, ((0,), (0,)))
            q = exact_dot(sin, part, ((0,), (0,)))
            u[k, :, 0:LANES] = p[:, 0:LANES] + q[:, LANES:]
            u[k, :, LANES:W] = p[:, LANES:] - q[:, 0:LANES]

        for i, (start, size) in enumerate(pieces if c == C - 1 else [(0, R)]):

            @pl.loop(0, size // 8)
            def _(t):
                rows = pl.ds(pl.multiple_of(start + t * 8, 8), 8)
                values = [(u[k, rows, 0:LANES], u[k, rows, LANES:W]) for k in range(F)]
                for q, (re, im) in enumerate(block_dft(values, 1.0)):
                    sendy[q, rows, c * W:c * W + LANES] = re
                    sendy[q, rows, c * W + LANES:(c + 1) * W] = im

            span = pl.ds(start, size)
            for o in order:
                d = lax.rem(me + o, F)
                copy = pltpu.make_async_remote_copy(
                    src_ref=sendy.at[d, span, wide], dst_ref=recvy.at[me, span, wide],
                    send_sem=bs.at[c, i, o], recv_sem=br.at[c, i, o],
                    device_id={"facet": d}, device_id_type=pl.DeviceIdType.MESH,
                )
                copy.start()
                back[i].append(copy)
            copy = pltpu.make_async_copy(
                sendy.at[me, span, wide], recvy.at[me, span, wide], br.at[c, i, 0]
            )
            copy.start()
            back[i].append(copy)

    last = []
    for h, (start, size) in enumerate(pieces):
        for copy in back[h]:
            copy.wait()

        @pl.loop(0, size // 8)
        def _(t):
            rows = pl.ds(pl.multiple_of(start + t * 8, 8), 8)
            target = pl.ds(pl.multiple_of(t * 8, 8), 8)
            for c in range(C):
                re_at, im_at = pl.ds(c * W, LANES), pl.ds(c * W + LANES, LANES)
                values = [(recvy[j, rows, re_at], recvy[j, rows, im_at]) for j in range(F)]
                for b, (re, im) in enumerate(block_dft(values, 1.0)):
                    z[b, target, re_at] = re
                    z[b, target, im_at] = im

        span = pl.ds(start, size)

        @pl.loop(0, F)
        def _(b):
            line = exact_dot((t_ref[0, b], t_ref[1, b]), halves(z[b]), ((1,), (1,)))
            gt[pl.ds(b, A, stride=F), :] = line * scale

        for j in range(N // LANES):
            g[span, j * LANES:(j + 1) * LANES] = gt[j * LANES:(j + 1) * LANES, :].T[0:size, :]
        if h == 0:
            for o in range(CH):
                d = lax.rem(mine + o, CH)
                copy = halo_copy(
                    g.at[0:8, pl.ds(pl.multiple_of(d * T, LANES), T)], lowg_ref.at[mine],
                    gs.at[o], gr.at[o], {"chan": d, "facet": above},
                )
                copy.start()
                last.append(copy)
        for o in range(1, CH):
            d = lax.rem(mine + o, CH)
            e = lax.rem(mine + o + 1, CH)
            copy = halo_copy(
                g.at[span, pl.ds(pl.multiple_of(e * T, LANES), LANES)],
                rightg_ref.at[mine, span], rs.at[h, o], rr.at[h, o], {"chan": d},
            )
            copy.start()
            last.append(copy)
            copy = pltpu.make_async_remote_copy(
                src_ref=g.at[span, pl.ds(pl.multiple_of(d * T, LANES), T)],
                dst_ref=grad_ref.at[mine, span],
                send_sem=cs.at[h, o], recv_sem=cr.at[h, o],
                device_id={"chan": d}, device_id_type=pl.DeviceIdType.MESH,
            )
            copy.start()
            last.append(copy)
        copy = pltpu.make_async_copy(
            g.at[span, pl.ds(pl.multiple_of(mine * T, LANES), T)],
            grad_ref.at[mine, span], ls.at[1 + h],
        )
        copy.start()
        last.append(copy)
        copy = pltpu.make_async_copy(
            g.at[span, pl.ds(pl.multiple_of(after * T, LANES), LANES)],
            rightg_ref.at[mine, span], rr.at[h, 0],
        )
        copy.start()
        last.append(copy)
    for copy in edges + last:
        copy.wait()


def gradient_tiles(F, CH, image, weights, measured, dual):
    R, N = image.shape
    A = N // F
    C = A // LANES
    RC = R // LANES
    seed, turn = (jnp.asarray(t) for t in table_seeds(F, A))
    PC = len(back_pieces(R))
    T = N // CH
    tile = jax.ShapeDtypeStruct((CH, R, T), jnp.float32)
    line = jax.ShapeDtypeStruct((CH, 8, T), jnp.float32)
    side = jax.ShapeDtypeStruct((CH, R, LANES), jnp.float32)
    f32 = jnp.float32
    dma = pltpu.SemaphoreType.DMA
    vmem = pl.BlockSpec(memory_space=pltpu.VMEM)
    hbm = pl.BlockSpec(memory_space=pl.ANY)
    return pl.pallas_call(
        partial(kernel, F, CH),
        out_shape=(tile, tile, line, side, line, line, side, side),
        in_specs=[vmem, vmem, vmem, hbm, hbm, hbm],
        out_specs=(hbm,) * 8,
        scratch_shapes=[
            pltpu.VMEM((2, F, A, 2 * A), jnp.bfloat16),
            pltpu.VMEM((CH, R, T), f32),
            pltpu.VMEM((CH, 8, T), f32),
            pltpu.VMEM((CH, R, LANES), f32),
            pltpu.VMEM((CH, 2, R, T), jnp.bfloat16),
            pltpu.VMEM((CH, 8, T), f32),
            pltpu.VMEM((CH, R, LANES), f32),
            pltpu.VMEM((CH, 8, T), f32),
            pltpu.VMEM((CH, R, LANES), f32),
            pltpu.VMEM((RC, N, LANES), f32),
            pltpu.VMEM((F, LANES, 2 * A), f32),
            pltpu.VMEM((C, F, R, 2 * LANES), f32),
            pltpu.VMEM((C, F, R, 2 * LANES), f32),
            pltpu.VMEM((N, A), jnp.bfloat16),
            pltpu.VMEM((2, N, A), jnp.bfloat16),
            pltpu.VMEM((C, N, LANES), f32),
            pltpu.VMEM((C, 2, N, LANES), f32),
            pltpu.VMEM((F, A, 2 * LANES), f32),
            pltpu.VMEM((F, R, 2 * A), f32),
            pltpu.VMEM((F, R, 2 * A), f32),
            pltpu.VMEM((N, LANES), f32),
            pltpu.VMEM((R, N), f32),
            dma((6,)),
            dma((C, RC, F)), dma((C, RC, F)),
            dma((C, PC, F)), dma((C, PC, F)),
            dma((PC, CH)), dma((PC, CH)),
            dma((CH,)), dma((CH,)),
            dma((1 + PC,)),
            dma((4,)), dma((4,)),
            dma((PC, CH)), dma((PC, CH)),
            dma((CH,)), dma((CH,)),
        ],
        compiler_params=pltpu.CompilerParams(
            collective_id=0, has_side_effects=True, vmem_limit_bytes=60 * 1024 * 1024
        ),
    )(image, seed, turn, weights, measured, dual)


def prior_kernel(
    n, edge, x, g, d, up, left, low, lowg, right, rightg, image, dual, ext, held, carry, parts
):
    t = pl.program_id(0)
    CH, TR, T = x.shape
    now = lax.rem(t, 2)
    row = lax.broadcasted_iota(jnp.int32, (TR, T), 0)
    lane = lax.broadcasted_iota(jnp.int32, (TR, T), 1)

    @pl.when(t == 0)
    def _():
        carry[...] = jnp.where(edge[0] == 0, 0.0, up[...])

    @pl.when(t < n)
    def _():
        for c in range(CH):
            p = d[c, 0].astype(jnp.float32)
            q = d[c, 1].astype(jnp.float32)
            p_prev = jnp.where(row == 0, carry[c, 7:8, :], pltpu.roll(p, 1, 0))
            first = jnp.where(edge[2] == 0, 0.0, left[c])[:, LANES - 1:LANES]
            q_prev = jnp.where(lane == 0, first, pltpu.roll(q, 1, 1))
            adjoint = p_prev - p + q_prev - q
            value = x[c] - step_primal * (g[c] + adjoint)
            image[c] = value
            ext[now, c] = 2.0 * value - x[c]
            held[now, c, 0] = p
            held[now, c, 1] = q
            carry[c] = p[TR - 8:TR, :]

    @pl.when(t > 0)
    def _():
        was = 1 - now
        total = jnp.zeros((TR, T), jnp.float32)
        for c in range(CH):
            e = ext[was, c]
            beyond = jnp.where(edge[1] == 0, 0.0, low[c] - lowg[c])
            following = jnp.where(t < n, ext[now, c, 0:8, :], beyond)[0:1, :]
            rows = jnp.where(row == TR - 1, following, pltpu.roll(e, TR - 1, 0)) - e
            side = jnp.where(edge[3] == 0, 0.0, right[c] - rightg[c])[:, 0:1]
            cols = jnp.where(lane == T - 1, side, pltpu.roll(e, T - 1, 1)) - e
            first_part = held[was, c, 0] + step_dual * rows
            second_part = held[was, c, 1] + step_dual * cols
            parts[c, 0] = first_part
            parts[c, 1] = second_part
            total = total + (first_part * first_part + second_part * second_part)
        factor = 1.0 / jnp.maximum(1.0, jnp.sqrt(total) / clip_radius)
        for c in range(CH):
            dual[c, 0] = (parts[c, 0] * factor).astype(jnp.bfloat16)
            dual[c, 1] = (parts[c, 1] * factor).astype(jnp.bfloat16)


def prior(edge, x, g, dual, up, left, low, lowg, right, rightg):
    CH, R, T = x.shape
    TR = 32
    n = R // TR
    f32 = jnp.float32
    ahead = lambda t: jnp.minimum(t, n - 1)
    behind = lambda t: jnp.maximum(t - 1, 0)
    tile = pl.BlockSpec((CH, TR, T), lambda t: (0, ahead(t), 0))
    line = pl.BlockSpec((CH, 8, T), lambda t: (0, 0, 0))
    return pl.pallas_call(
        partial(prior_kernel, n),
        grid=(n + 1,),
        out_shape=(
            jax.ShapeDtypeStruct((CH, R, T), f32),
            jax.ShapeDtypeStruct((CH, 2, R, T), jnp.bfloat16),
        ),
        in_specs=[
            pl.BlockSpec(memory_space=pltpu.SMEM),
            tile,
            tile,
            pl.BlockSpec((CH, 2, TR, T), lambda t: (0, 0, ahead(t), 0)),
            line,
            pl.BlockSpec((CH, TR, LANES), lambda t: (0, ahead(t), 0)),
            line,
            line,
            pl.BlockSpec((CH, TR, LANES), lambda t: (0, behind(t), 0)),
            pl.BlockSpec((CH, TR, LANES), lambda t: (0, behind(t), 0)),
        ],
        out_specs=(tile, pl.BlockSpec((CH, 2, TR, T), lambda t: (0, 0, behind(t), 0))),
        scratch_shapes=[
            pltpu.VMEM((2, CH, TR, T), f32),
            pltpu.VMEM((2, CH, 2, TR, T), f32),
            pltpu.VMEM((CH, 8, T), f32),
            pltpu.VMEM((CH, 2, TR, T), f32),
        ],
        compiler_params=pltpu.CompilerParams(vmem_limit_bytes=24 * 1024 * 1024),
    )(edge, x, g, dual, up, left, low, lowg, right, rightg)


def shards(image_field, weights, measured, dual_field):
    F, CH = lax.axis_size("facet"), lax.axis_size("chan")
    tiles = gradient_tiles(F, CH, image_field[0], weights, measured, dual_field)
    f, c = lax.axis_index("facet"), lax.axis_index("chan")
    edge = jnp.stack([f > 0, f < F - 1, c > 0, c < CH - 1]).astype(jnp.int32)
    return prior(edge, tiles[0], tiles[1], dual_field, *tiles[2:])


def solution(mesh):
    placed = (
        P("chan", "facet", None),
        P("chan", None, "facet"),
        P("chan", None, None, "facet"),
        P(None, None, "facet", "chan"),
    )
    return jax.shard_map(
        shards,
        mesh=mesh,
        in_specs=placed,
        out_specs=(P(None, "facet", "chan"), P(None, None, "facet", "chan")),
        check_vma=False,
    )
```

```python
from functools import partial
import math

import jax
import jax.numpy as jnp
import numpy as np
from jax import lax
from jax.experimental import pallas as pl
from jax.experimental.pallas import tpu as pltpu
from jax.sharding import PartitionSpec as P

step_primal = 0.5
step_dual = 0.5
clip_radius = 4.0
LANES = 128


def turned(real, imag, num, den, sign):
    num = num % den
    if num == 0:
        return real, imag
    if 4 * num == den:
        return (-imag, real) if sign > 0 else (imag, -real)
    c = math.cos(2.0 * math.pi * num / den)
    s = sign * math.sin(2.0 * math.pi * num / den)
    if 8 * num == den:
        h = math.sqrt(0.5)
        if sign > 0:
            return (real - imag) * h, (real + imag) * h
        return (real + imag) * h, (imag - real) * h
    return real * c - imag * s, real * s + imag * c


def block_dft(values, sign):
    n = len(values)
    if n == 1:
        return values
    even = block_dft(values[0::2], sign)
    odd = block_dft(values[1::2], sign)
    low, high = [], []
    for k in range(n // 2):
        er, ei = even[k]
        tr, ti = turned(*odd[k], k, n, sign)
        low.append((er + tr, ei + ti))
        high.append((er - tr, ei - ti))
    return low + high


def halves(x):
    high = x.astype(jnp.bfloat16)
    return high, (x - high.astype(jnp.float32)).astype(jnp.bfloat16)


def exact_dot(first, second, dims):
    (fh, fl), (sh, sl) = first, second
    dot = partial(
        lax.dot_general, dimension_numbers=(dims, ((), ())), preferred_element_type=jnp.float32
    )
    return dot(fh, sh) + (dot(fh, sl) + dot(fl, sh))


def table_seeds(blocks, inner):
    n = blocks * inner
    a = np.arange(max(blocks, inner))[:, None]
    i = np.arange(inner)[None, :]

    def pairs(step, count):
        phase = 2.0 * np.pi / n * ((step * a[:count] * i) % n)
        pair = np.stack([np.cos(phase), -np.sin(phase)], axis=1).astype(np.float32)
        pair = pair.reshape(count, 2, inner // LANES, LANES)
        return pair.transpose(0, 2, 1, 3).reshape(count, 2 * inner)

    return pairs(blocks, inner), np.repeat(pairs(1, blocks)[:, None, :], 8, axis=1)


def fill_tables(seed_ref, turn_ref, t_ref):
    _, F, A, width = t_ref.shape

    @pl.loop(0, F)
    def _(b):
        for c in range(width // (2 * LANES)):
            re_at = slice(2 * c * LANES, (2 * c + 1) * LANES)
            im_at = slice((2 * c + 1) * LANES, (2 * c + 2) * LANES)
            turn_re, turn_im = turn_ref[b, 0:1, re_at], turn_ref[b, 0:1, im_at]

            @pl.loop(0, A // 32)
            def _(t):
                rows = pl.ds(pl.multiple_of(t * 32, 32), 32)
                re, im = seed_ref[rows, re_at], seed_ref[rows, im_at]
                pair = (re * turn_re - im * turn_im, re * turn_im + im * turn_re)
                for value, at in zip(pair, (re_at, im_at)):
                    high, low = halves(value)
                    t_ref[0, b, rows, at] = high
                    t_ref[1, b, rows, at] = low


def back_pieces(rows):
    pieces, start = [], 0
    while rows - start > 32:
        size = min(LANES, (rows - start) // 2)
        pieces.append((start, size))
        start += size
    return pieces + [(start, rows - start)]


def square_tables(t_ref, k, chunks):
    found = []
    for at in (0, LANES):
        pieces = [
            [t_ref[s, k, :, 2 * LANES * c + at:2 * LANES * c + at + LANES] for c in range(chunks)]
            for s in (0, 1)
        ]
        found.append(tuple(jnp.concatenate(p, axis=1) if chunks > 1 else p[0] for p in pieces))
    return found


def halo_copy(source, target, send_sem, recv_sem, device):
    return pltpu.make_async_remote_copy(
        src_ref=source, dst_ref=target, send_sem=send_sem, recv_sem=recv_sem,
        device_id=device, device_id_type=pl.DeviceIdType.MESH,
    )


def kernel(
    F, CH, x_ref, seed_ref, turn_ref, w_hbm, m_hbm, d_hbm,
    image_hbm, grad_ref, up_hbm, left_hbm, low_ref, lowg_ref, right_ref, rightg_ref,
    t_ref, image_ref, up_ref, left_ref, dual, up, left, low, right,
    xt, z, send, recv, wb, mb, wf, mf, u, sendy, recvy, gt, g,
    in_sem, fs, fr, bs, br, cs, cr, xs, xr, ls, hs, hr, rs, rr, gs, gr,
):
    R, N = x_ref.shape
    A = N // F
    C = A // LANES
    T = N // CH
    RC = R // LANES
    W = 2 * LANES
    scale = 1.0 / N
    me = lax.axis_index("facet")
    mine = lax.axis_index("chan")
    order = sorted(range(1, F), key=lambda o: abs(o - F // 2))

    load_w = pltpu.make_async_copy(w_hbm.at[0], wb, in_sem.at[0])
    load_m = pltpu.make_async_copy(m_hbm.at[0], mb, in_sem.at[1])
    load_w.start()
    load_m.start()
    load_d = pltpu.make_async_copy(d_hbm, dual, in_sem.at[2])
    load_d.start()
    above, below = lax.rem(me + F - 1, F), lax.rem(me + 1, F)
    before, after = lax.rem(mine + CH - 1, CH), lax.rem(mine + 1, CH)

    barrier = pltpu.get_barrier_semaphore()
    for o in range(1, F):
        pl.semaphore_signal(
            barrier, inc=1, device_id={"facet": lax.rem(me + o, F)},
            device_id_type=pl.DeviceIdType.MESH,
        )
    for o in range(1, CH):
        pl.semaphore_signal(
            barrier, inc=1, device_id={"chan": lax.rem(mine + o, CH)},
            device_id_type=pl.DeviceIdType.MESH,
        )
        for f in (above, below):
            pl.semaphore_signal(
                barrier, inc=1, device_id={"chan": lax.rem(mine + o, CH), "facet": f},
                device_id_type=pl.DeviceIdType.MESH,
            )
    fill_tables(seed_ref, turn_ref, t_ref)
    load_d.wait()
    for k in range(CH):
        up[k] = dual[k, 0, R - 16:R, :].astype(jnp.float32)[8:16, :]
        left[k] = dual[k, 1, :, T - LANES:T].astype(jnp.float32)
    pl.semaphore_wait(barrier, F - 1 + 3 * (CH - 1))

    halos = [
        halo_copy(up, up_ref, hs.at[0], hr.at[0], {"facet": below}),
        halo_copy(left, left_ref, hs.at[1], hr.at[1], {"chan": after}),
    ]
    for copy in halos:
        copy.start()

    image_copies = []
    for o in range(1, CH):
        d = lax.rem(mine + o, CH)
        copy = pltpu.make_async_remote_copy(
            src_ref=x_ref.at[:, pl.ds(pl.multiple_of(d * T, LANES), T)],
            dst_ref=image_ref.at[mine],
            send_sem=xs.at[o], recv_sem=xr.at[o],
            device_id={"chan": d}, device_id_type=pl.DeviceIdType.MESH,
        )
        copy.start()
        image_copies.append(copy)
    own = pltpu.make_async_copy(
        x_ref.at[:, pl.ds(pl.multiple_of(mine * T, LANES), T)], image_ref.at[mine], ls.at[0]
    )
    own.start()
    image_copies.append(own)

    copies = []
    for c in range(C):
        wide = slice(c * W, (c + 1) * W)
        group = []
        for h in range(RC):
            if c == 0:
                for j in range(N // LANES):
                    xt[h, j * LANES:(j + 1) * LANES, :] = x_ref[
                        h * LANES:(h + 1) * LANES, j * LANES:(j + 1) * LANES
                    ].T

            @pl.loop(0, F)
            def _(b):
                part = halves(xt[h, pl.ds(b, A, stride=F), :].T)
                table = (t_ref[0, b, :, wide], t_ref[1, b, :, wide])
                z[b, 0:LANES, 0:W] = exact_dot(part, table, ((1,), (0,)))

            @pl.loop(0, LANES // 8)
            def _(t):
                rows = pl.ds(pl.multiple_of(t * 8, 8), 8)
                target = pl.ds(pl.multiple_of(h * LANES + t * 8, 8), 8)
                values = [(z[b, rows, 0:LANES], z[b, rows, LANES:W]) for b in range(F)]
                for j, (re, im) in enumerate(block_dft(values, -1.0)):
                    send[c, j, target, 0:LANES] = re
                    send[c, j, target, LANES:W] = im

            span = pl.ds(h * LANES, LANES)
            for o in order:
                d = lax.rem(me + o, F)
                copy = pltpu.make_async_remote_copy(
                    src_ref=send.at[c, d, span], dst_ref=recv.at[c, me, span],
                    send_sem=fs.at[c, h, o], recv_sem=fr.at[c, h, o],
                    device_id={"facet": d}, device_id_type=pl.DeviceIdType.MESH,
                )
                copy.start()
                group.append(copy)
            copy = pltpu.make_async_copy(
                send.at[c, me, span], recv.at[c, me, span], fr.at[c, h, 0]
            )
            copy.start()
            group.append(copy)
        copies.append(group)

    load_w.wait()
    load_m.wait()

    @pl.loop(0, N // 16)
    def _(t):
        rows = pl.ds(pl.multiple_of(t * 16, 16), 16)
        for c in range(C):
            lo = c * LANES
            wf[c, rows, :] = wb[rows, lo:lo + LANES].astype(jnp.float32) * scale
            mf[c, 0, rows, :] = mb[0, rows, lo:lo + LANES].astype(jnp.float32)
            mf[c, 1, rows, :] = mb[1, rows, lo:lo + LANES].astype(jnp.float32)

    pieces = back_pieces(R)
    back = [[] for _ in pieces]
    for c in range(C):
        wide = slice(c * W, (c + 1) * W)
        for copy in copies[c]:
            copy.wait()

        @pl.loop(0, R // 8)
        def _(t):
            rows = pl.ds(pl.multiple_of(t * 8, 8), 8)
            values = [(recv[c, q, rows, 0:LANES], recv[c, q, rows, LANES:W]) for q in range(F)]
            for k, (re, im) in enumerate(block_dft(values, -1.0)):
                u[k, rows, 0:LANES] = re
                u[k, rows, LANES:W] = im

        @pl.loop(0, F)
        def _(k):
            cos, sin = square_tables(t_ref, k, C)
            part = halves(u[k])
            p = exact_dot(cos, part, ((1,), (0,)))
            q = exact_dot(sin, part, ((1,), (0,)))
            spec_re = p[:, 0:LANES] - q[:, LANES:]
            spec_im = p[:, LANES:] + q[:, 0:LANES]
            lines = pl.ds(k, A, stride=F)
            weight = wf[c, lines, :]
            res_re = weight * spec_re - mf[c, 0, lines, :]
            res_im = weight * spec_im - mf[c, 1, lines, :]
            part = halves(jnp.concatenate([res_re, res_im], axis=1))
            p = exact_dot(cos, part, ((0,), (0,)))
            q = exact_dot(sin, part, ((0,), (0,)))
            u[k, :, 0:LANES] = p[:, 0:LANES] + q[:, LANES:]
            u[k, :, LANES:W] = p[:, LANES:] - q[:, 0:LANES]

        for i, (start, size) in enumerate(pieces if c == C - 1 else [(0, R)]):

            @pl.loop(0, size // 8)
            def _(t):
                rows = pl.ds(pl.multiple_of(start + t * 8, 8), 8)
                values = [(u[k, rows, 0:LANES], u[k, rows, LANES:W]) for k in range(F)]
                for q, (re, im) in enumerate(block_dft(values, 1.0)):
                    sendy[q, rows, c * W:c * W + LANES] = re
                    sendy[q, rows, c * W + LANES:(c + 1) * W] = im

            span = pl.ds(start, size)
            for o in order:
                d = lax.rem(me + o, F)
                copy = pltpu.make_async_remote_copy(
                    src_ref=sendy.at[d, span, wide], dst_ref=recvy.at[me, span, wide],
                    send_sem=bs.at[c, i, o], recv_sem=br.at[c, i, o],
                    device_id={"facet": d}, device_id_type=pl.DeviceIdType.MESH,
                )
                copy.start()
                back[i].append(copy)
            copy = pltpu.make_async_copy(
                sendy.at[me, span, wide], recvy.at[me, span, wide], br.at[c, i, 0]
            )
            copy.start()
            back[i].append(copy)

        if c == 0:
            for copy in image_copies + halos:
                copy.wait()
            edges = [
                pltpu.make_async_copy(image_ref, image_hbm, in_sem.at[3]),
                pltpu.make_async_copy(up_ref, up_hbm, in_sem.at[4]),
                pltpu.make_async_copy(left_ref, left_hbm, in_sem.at[5]),
            ]
            for k in range(CH):
                first_up = jnp.where(me > 0, up_ref[k], 0.0)[7:8, :]
                first_left = jnp.where(mine > 0, left_ref[k], 0.0)[:, LANES - 1:LANES]
                p = dual[k, 0, 0:16, :].astype(jnp.float32)[0:8, :]
                q = dual[k, 1, 0:16, :].astype(jnp.float32)[0:8, :]
                lane = lax.broadcasted_iota(jnp.int32, (8, T), 1)
                q_prev = jnp.where(lane == 0, first_left[0:8, :], pltpu.roll(q, 1, 1))
                low[k] = image_ref[k, 0:8, :] - (first_up - p + q_prev - q)
                p = dual[k, 0, :, 0:LANES].astype(jnp.float32)
                q = dual[k, 1, :, 0:LANES].astype(jnp.float32)
                row = lax.broadcasted_iota(jnp.int32, (R, LANES), 0)
                p_prev = jnp.where(row == 0, first_up[:, 0:LANES], pltpu.roll(p, 1, 0))
                right[k] = image_ref[k, :, 0:LANES] - (p_prev - p + first_left - q)
            edges += [
                halo_copy(low, low_ref, hs.at[2], hr.at[2], {"facet": above}),
                halo_copy(right, right_ref, hs.at[3], hr.at[3], {"chan": before}),
            ]
            for copy in edges:
                copy.start()

    last = []
    for h, (start, size) in enumerate(pieces):
        for copy in back[h]:
            copy.wait()

        @pl.loop(0, size // 8)
        def _(t):
            rows = pl.ds(pl.multiple_of(start + t * 8, 8), 8)
            target = pl.ds(pl.multiple_of(t * 8, 8), 8)
            for c in range(C):
                re_at, im_at = pl.ds(c * W, LANES), pl.ds(c * W + LANES, LANES)
                values = [(recvy[j, rows, re_at], recvy[j, rows, im_at]) for j in range(F)]
                for b, (re, im) in enumerate(block_dft(values, 1.0)):
                    z[b, target, re_at] = re
                    z[b, target, im_at] = im

        span = pl.ds(start, size)

        @pl.loop(0, F)
        def _(b):
            line = exact_dot((t_ref[0, b], t_ref[1, b]), halves(z[b]), ((1,), (1,)))
            gt[pl.ds(b, A, stride=F), :] = line * scale

        for j in range(N // LANES):
            g[span, j * LANES:(j + 1) * LANES] = gt[j * LANES:(j + 1) * LANES, :].T[0:size, :]
        if h == 0:
            for o in range(CH):
                d = lax.rem(mine + o, CH)
                copy = halo_copy(
                    g.at[0:8, pl.ds(pl.multiple_of(d * T, LANES), T)], lowg_ref.at[mine],
                    gs.at[o], gr.at[o], {"chan": d, "facet": above},
                )
                copy.start()
                last.append(copy)
        for o in range(1, CH):
            d = lax.rem(mine + o, CH)
            e = lax.rem(mine + o + 1, CH)
            copy = halo_copy(
                g.at[span, pl.ds(pl.multiple_of(e * T, LANES), LANES)],
                rightg_ref.at[mine, span], rs.at[h, o], rr.at[h, o], {"chan": d},
            )
            copy.start()
            last.append(copy)
            copy = pltpu.make_async_remote_copy(
                src_ref=g.at[span, pl.ds(pl.multiple_of(d * T, LANES), T)],
                dst_ref=grad_ref.at[mine, span],
                send_sem=cs.at[h, o], recv_sem=cr.at[h, o],
                device_id={"chan": d}, device_id_type=pl.DeviceIdType.MESH,
            )
            copy.start()
            last.append(copy)
        copy = pltpu.make_async_copy(
            g.at[span, pl.ds(pl.multiple_of(mine * T, LANES), T)],
            grad_ref.at[mine, span], ls.at[1 + h],
        )
        copy.start()
        last.append(copy)
        copy = pltpu.make_async_copy(
            g.at[span, pl.ds(pl.multiple_of(after * T, LANES), LANES)],
            rightg_ref.at[mine, span], rr.at[h, 0],
        )
        copy.start()
        last.append(copy)
    for copy in edges + last:
        copy.wait()


def gradient_tiles(F, CH, image, weights, measured, dual):
    R, N = image.shape
    A = N // F
    C = A // LANES
    RC = R // LANES
    seed, turn = (jnp.asarray(t) for t in table_seeds(F, A))
    PC = len(back_pieces(R))
    T = N // CH
    tile = jax.ShapeDtypeStruct((CH, R, T), jnp.float32)
    line = jax.ShapeDtypeStruct((CH, 8, T), jnp.float32)
    side = jax.ShapeDtypeStruct((CH, R, LANES), jnp.float32)
    f32 = jnp.float32
    dma = pltpu.SemaphoreType.DMA
    vmem = pl.BlockSpec(memory_space=pltpu.VMEM)
    hbm = pl.BlockSpec(memory_space=pl.ANY)
    return pl.pallas_call(
        partial(kernel, F, CH),
        out_shape=(tile, tile, line, side, line, line, side, side),
        in_specs=[vmem, vmem, vmem, hbm, hbm, hbm],
        out_specs=(hbm,) * 8,
        scratch_shapes=[
            pltpu.VMEM((2, F, A, 2 * A), jnp.bfloat16),
            pltpu.VMEM((CH, R, T), f32),
            pltpu.VMEM((CH, 8, T), f32),
            pltpu.VMEM((CH, R, LANES), f32),
            pltpu.VMEM((CH, 2, R, T), jnp.bfloat16),
            pltpu.VMEM((CH, 8, T), f32),
            pltpu.VMEM((CH, R, LANES), f32),
            pltpu.VMEM((CH, 8, T), f32),
            pltpu.VMEM((CH, R, LANES), f32),
            pltpu.VMEM((RC, N, LANES), f32),
            pltpu.VMEM((F, LANES, 2 * A), f32),
            pltpu.VMEM((C, F, R, 2 * LANES), f32),
            pltpu.VMEM((C, F, R, 2 * LANES), f32),
            pltpu.VMEM((N, A), jnp.bfloat16),
            pltpu.VMEM((2, N, A), jnp.bfloat16),
            pltpu.VMEM((C, N, LANES), f32),
            pltpu.VMEM((C, 2, N, LANES), f32),
            pltpu.VMEM((F, A, 2 * LANES), f32),
            pltpu.VMEM((F, R, 2 * A), f32),
            pltpu.VMEM((F, R, 2 * A), f32),
            pltpu.VMEM((N, LANES), f32),
            pltpu.VMEM((R, N), f32),
            dma((6,)),
            dma((C, RC, F)), dma((C, RC, F)),
            dma((C, PC, F)), dma((C, PC, F)),
            dma((PC, CH)), dma((PC, CH)),
            dma((CH,)), dma((CH,)),
            dma((1 + PC,)),
            dma((4,)), dma((4,)),
            dma((PC, CH)), dma((PC, CH)),
            dma((CH,)), dma((CH,)),
        ],
        compiler_params=pltpu.CompilerParams(
            collective_id=0, has_side_effects=True, vmem_limit_bytes=60 * 1024 * 1024
        ),
    )(image, seed, turn, weights, measured, dual)


def prior_kernel(
    n, edge, x, g, d, up, left, low, lowg, right, rightg, image, dual, ext, held, carry, parts
):
    t = pl.program_id(0)
    CH, TR, T = x.shape
    now = lax.rem(t, 2)
    row = lax.broadcasted_iota(jnp.int32, (TR, T), 0)
    lane = lax.broadcasted_iota(jnp.int32, (TR, T), 1)

    @pl.when(t == 0)
    def _():
        carry[...] = jnp.where(edge[0] == 0, 0.0, up[...])

    @pl.when(t < n)
    def _():
        for c in range(CH):
            p = d[c, 0].astype(jnp.float32)
            q = d[c, 1].astype(jnp.float32)
            p_prev = jnp.where(row == 0, carry[c, 7:8, :], pltpu.roll(p, 1, 0))
            first = jnp.where(edge[2] == 0, 0.0, left[c])[:, LANES - 1:LANES]
            q_prev = jnp.where(lane == 0, first, pltpu.roll(q, 1, 1))
            adjoint = p_prev - p + q_prev - q
            value = x[c] - step_primal * (g[c] + adjoint)
            image[c] = value
            ext[now, c] = 2.0 * value - x[c]
            held[now, c, 0] = p
            held[now, c, 1] = q
            carry[c] = p[TR - 8:TR, :]

    @pl.when(t > 0)
    def _():
        was = 1 - now
        total = jnp.zeros((TR, T), jnp.float32)
        for c in range(CH):
            e = ext[was, c]
            beyond = jnp.where(edge[1] == 0, 0.0, low[c] - lowg[c])
            following = jnp.where(t < n, ext[now, c, 0:8, :], beyond)[0:1, :]
            rows = jnp.where(row == TR - 1, following, pltpu.roll(e, TR - 1, 0)) - e
            side = jnp.where(edge[3] == 0, 0.0, right[c] - rightg[c])[:, 0:1]
            cols = jnp.where(lane == T - 1, side, pltpu.roll(e, T - 1, 1)) - e
            first_part = held[was, c, 0] + step_dual * rows
            second_part = held[was, c, 1] + step_dual * cols
            parts[c, 0] = first_part
            parts[c, 1] = second_part
            total = total + (first_part * first_part + second_part * second_part)
        factor = 1.0 / jnp.maximum(1.0, jnp.sqrt(total) / clip_radius)
        for c in range(CH):
            dual[c, 0] = (parts[c, 0] * factor).astype(jnp.bfloat16)
            dual[c, 1] = (parts[c, 1] * factor).astype(jnp.bfloat16)


def prior(edge, x, g, dual, up, left, low, lowg, right, rightg):
    CH, R, T = x.shape
    TR = 32
    n = R // TR
    f32 = jnp.float32
    ahead = lambda t: jnp.minimum(t, n - 1)
    behind = lambda t: jnp.maximum(t - 1, 0)
    tile = pl.BlockSpec((CH, TR, T), lambda t: (0, ahead(t), 0))
    line = pl.BlockSpec((CH, 8, T), lambda t: (0, 0, 0))
    return pl.pallas_call(
        partial(prior_kernel, n),
        grid=(n + 1,),
        out_shape=(
            jax.ShapeDtypeStruct((CH, R, T), f32),
            jax.ShapeDtypeStruct((CH, 2, R, T), jnp.bfloat16),
        ),
        in_specs=[
            pl.BlockSpec(memory_space=pltpu.SMEM),
            tile,
            tile,
            pl.BlockSpec((CH, 2, TR, T), lambda t: (0, 0, ahead(t), 0)),
            line,
            pl.BlockSpec((CH, TR, LANES), lambda t: (0, ahead(t), 0)),
            line,
            line,
            pl.BlockSpec((CH, TR, LANES), lambda t: (0, behind(t), 0)),
            pl.BlockSpec((CH, TR, LANES), lambda t: (0, behind(t), 0)),
        ],
        out_specs=(tile, pl.BlockSpec((CH, 2, TR, T), lambda t: (0, 0, behind(t), 0))),
        scratch_shapes=[
            pltpu.VMEM((2, CH, TR, T), f32),
            pltpu.VMEM((2, CH, 2, TR, T), f32),
            pltpu.VMEM((CH, 8, T), f32),
            pltpu.VMEM((CH, 2, TR, T), f32),
        ],
        compiler_params=pltpu.CompilerParams(vmem_limit_bytes=60 * 1024 * 1024),
    )(edge, x, g, dual, up, left, low, lowg, right, rightg)


def shards(image_field, weights, measured, dual_field):
    F, CH = lax.axis_size("facet"), lax.axis_size("chan")
    tiles = gradient_tiles(F, CH, image_field[0], weights, measured, dual_field)
    f, c = lax.axis_index("facet"), lax.axis_index("chan")
    edge = jnp.stack([f > 0, f < F - 1, c > 0, c < CH - 1]).astype(jnp.int32)
    return prior(edge, tiles[0], tiles[1], dual_field, *tiles[2:])


def solution(mesh):
    placed = (
        P("chan", "facet", None),
        P("chan", None, "facet"),
        P("chan", None, None, "facet"),
        P(None, None, "facet", "chan"),
    )
    return jax.shard_map(
        shards,
        mesh=mesh,
        in_specs=placed,
        out_specs=(P(None, "facet", "chan"), P(None, None, "facet", "chan")),
        check_vma=False,
    )
```

```python
from functools import partial
import math

import jax
import jax.numpy as jnp
import numpy as np
from jax import lax
from jax.experimental import pallas as pl
from jax.experimental.pallas import tpu as pltpu
from jax.sharding import PartitionSpec as P

step_primal = 0.5
step_dual = 0.5
clip_radius = 4.0
LANES = 128


def turned(real, imag, num, den, sign):
    num = num % den
    if num == 0:
        return real, imag
    if 4 * num == den:
        return (-imag, real) if sign > 0 else (imag, -real)
    c = math.cos(2.0 * math.pi * num / den)
    s = sign * math.sin(2.0 * math.pi * num / den)
    if 8 * num == den:
        h = math.sqrt(0.5)
        if sign > 0:
            return (real - imag) * h, (real + imag) * h
        return (real + imag) * h, (imag - real) * h
    return real * c - imag * s, real * s + imag * c


def block_dft(values, sign):
    n = len(values)
    if n == 1:
        return values
    even = block_dft(values[0::2], sign)
    odd = block_dft(values[1::2], sign)
    low, high = [], []
    for k in range(n // 2):
        er, ei = even[k]
        tr, ti = turned(*odd[k], k, n, sign)
        low.append((er + tr, ei + ti))
        high.append((er - tr, ei - ti))
    return low + high


def halves(x):
    high = x.astype(jnp.bfloat16)
    return high, (x - high.astype(jnp.float32)).astype(jnp.bfloat16)


def exact_dot(first, second, dims):
    (fh, fl), (sh, sl) = first, second
    dot = partial(
        lax.dot_general, dimension_numbers=(dims, ((), ())), preferred_element_type=jnp.float32
    )
    return dot(fh, sh) + (dot(fh, sl) + dot(fl, sh))


def table_seeds(blocks, inner):
    n = blocks * inner
    a = np.arange(max(blocks, inner))[:, None]
    i = np.arange(inner)[None, :]

    def pairs(step, count):
        phase = 2.0 * np.pi / n * ((step * a[:count] * i) % n)
        pair = np.stack([np.cos(phase), -np.sin(phase)], axis=1).astype(np.float32)
        pair = pair.reshape(count, 2, inner // LANES, LANES)
        return pair.transpose(0, 2, 1, 3).reshape(count, 2 * inner)

    return pairs(blocks, inner), np.repeat(pairs(1, blocks)[:, None, :], 8, axis=1)


def fill_tables(seed_ref, turn_ref, t_ref):
    _, F, A, width = t_ref.shape

    @pl.loop(0, F)
    def _(b):
        for c in range(width // (2 * LANES)):
            re_at = slice(2 * c * LANES, (2 * c + 1) * LANES)
            im_at = slice((2 * c + 1) * LANES, (2 * c + 2) * LANES)
            turn_re, turn_im = turn_ref[b, 0:1, re_at], turn_ref[b, 0:1, im_at]

            @pl.loop(0, A // 32)
            def _(t):
                rows = pl.ds(pl.multiple_of(t * 32, 32), 32)
                re, im = seed_ref[rows, re_at], seed_ref[rows, im_at]
                pair = (re * turn_re - im * turn_im, re * turn_im + im * turn_re)
                for value, at in zip(pair, (re_at, im_at)):
                    high, low = halves(value)
                    t_ref[0, b, rows, at] = high
                    t_ref[1, b, rows, at] = low


def back_pieces(rows):
    pieces, start = [], 0
    while rows - start > 32:
        size = min(LANES, (rows - start) // 2)
        pieces.append((start, size))
        start += size
    return pieces + [(start, rows - start)]


def square_tables(t_ref, k, chunks):
    found = []
    for at in (0, LANES):
        pieces = [
            [t_ref[s, k, :, 2 * LANES * c + at:2 * LANES * c + at + LANES] for c in range(chunks)]
            for s in (0, 1)
        ]
        found.append(tuple(jnp.concatenate(p, axis=1) if chunks > 1 else p[0] for p in pieces))
    return found


def halo_copy(source, target, send_sem, recv_sem, device):
    return pltpu.make_async_remote_copy(
        src_ref=source, dst_ref=target, send_sem=send_sem, recv_sem=recv_sem,
        device_id=device, device_id_type=pl.DeviceIdType.MESH,
    )


def kernel(
    F, CH, x_ref, seed_ref, turn_ref, w_hbm, m_hbm, d_hbm,
    image_hbm, grad_ref, up_hbm, left_hbm, low_ref, lowg_ref, right_ref, rightg_ref,
    t_ref, image_ref, up_ref, left_ref, dual, up, left, low, right,
    xt, z, send, recv, wb, mb, wf, mf, u, sendy, recvy, gt, g,
    in_sem, fs, fr, bs, br, cs, cr, xs, xr, ls, hs, hr, rs, rr, gs, gr,
):
    R, N = x_ref.shape
    A = N // F
    C = A // LANES
    T = N // CH
    RC = R // LANES
    W = 2 * LANES
    scale = 1.0 / N
    me = lax.axis_index("facet")
    mine = lax.axis_index("chan")
    order = sorted(range(1, F), key=lambda o: abs(o - F // 2))

    load_w = pltpu.make_async_copy(w_hbm.at[0], wb, in_sem.at[0])
    load_m = pltpu.make_async_copy(m_hbm.at[0], mb, in_sem.at[1])
    load_w.start()
    load_m.start()
    load_d = pltpu.make_async_copy(d_hbm, dual, in_sem.at[2])
    load_d.start()
    above, below = lax.rem(me + F - 1, F), lax.rem(me + 1, F)
    before, after = lax.rem(mine + CH - 1, CH), lax.rem(mine + 1, CH)

    barrier = pltpu.get_barrier_semaphore()
    for o in range(1, F):
        pl.semaphore_signal(
            barrier, inc=1, device_id={"facet": lax.rem(me + o, F)},
            device_id_type=pl.DeviceIdType.MESH,
        )
    for o in range(1, CH):
        pl.semaphore_signal(
            barrier, inc=1, device_id={"chan": lax.rem(mine + o, CH)},
            device_id_type=pl.DeviceIdType.MESH,
        )
        for f in (above, below):
            pl.semaphore_signal(
                barrier, inc=1, device_id={"chan": lax.rem(mine + o, CH), "facet": f},
                device_id_type=pl.DeviceIdType.MESH,
            )
    fill_tables(seed_ref, turn_ref, t_ref)
    load_d.wait()
    for k in range(CH):
        up[k] = dual[k, 0, R - 16:R, :].astype(jnp.float32)[8:16, :]
        left[k] = dual[k, 1, :, T - LANES:T].astype(jnp.float32)
    pl.semaphore_wait(barrier, F - 1 + 3 * (CH - 1))

    halos = [
        halo_copy(up, up_ref, hs.at[0], hr.at[0], {"facet": below}),
        halo_copy(left, left_ref, hs.at[1], hr.at[1], {"chan": after}),
    ]
    for copy in halos:
        copy.start()

    image_copies = []
    for o in range(1, CH):
        d = lax.rem(mine + o, CH)
        copy = pltpu.make_async_remote_copy(
            src_ref=x_ref.at[:, pl.ds(pl.multiple_of(d * T, LANES), T)],
            dst_ref=image_ref.at[mine],
            send_sem=xs.at[o], recv_sem=xr.at[o],
            device_id={"chan": d}, device_id_type=pl.DeviceIdType.MESH,
        )
        copy.start()
        image_copies.append(copy)
    own = pltpu.make_async_copy(
        x_ref.at[:, pl.ds(pl.multiple_of(mine * T, LANES), T)], image_ref.at[mine], ls.at[0]
    )
    own.start()
    image_copies.append(own)

    copies = []
    for c in range(C):
        wide = slice(c * W, (c + 1) * W)
        group = []
        for h in range(RC):
            if c == 0:
                for j in range(N // LANES):
                    xt[h, j * LANES:(j + 1) * LANES, :] = x_ref[
                        h * LANES:(h + 1) * LANES, j * LANES:(j + 1) * LANES
                    ].T

            @pl.loop(0, F)
            def _(b):
                part = halves(xt[h, pl.ds(b, A, stride=F), :].T)
                table = (t_ref[0, b, :, wide], t_ref[1, b, :, wide])
                z[b, 0:LANES, 0:W] = exact_dot(part, table, ((1,), (0,)))

            @pl.loop(0, LANES // 8)
            def _(t):
                rows = pl.ds(pl.multiple_of(t * 8, 8), 8)
                target = pl.ds(pl.multiple_of(h * LANES + t * 8, 8), 8)
                values = [(z[b, rows, 0:LANES], z[b, rows, LANES:W]) for b in range(F)]
                for j, (re, im) in enumerate(block_dft(values, -1.0)):
                    send[c, j, target, 0:LANES] = re
                    send[c, j, target, LANES:W] = im

            span = pl.ds(h * LANES, LANES)
            for o in order:
                d = lax.rem(me + o, F)
                copy = pltpu.make_async_remote_copy(
                    src_ref=send.at[c, d, span], dst_ref=recv.at[c, me, span],
                    send_sem=fs.at[c, h, o], recv_sem=fr.at[c, h, o],
                    device_id={"facet": d}, device_id_type=pl.DeviceIdType.MESH,
                )
                copy.start()
                group.append(copy)
            copy = pltpu.make_async_copy(
                send.at[c, me, span], recv.at[c, me, span], fr.at[c, h, 0]
            )
            copy.start()
            group.append(copy)
        copies.append(group)

    load_w.wait()
    load_m.wait()

    @pl.loop(0, N // 16)
    def _(t):
        rows = pl.ds(pl.multiple_of(t * 16, 16), 16)
        for c in range(C):
            lo = c * LANES
            wf[c, rows, :] = wb[rows, lo:lo + LANES].astype(jnp.float32) * scale
            mf[c, 0, rows, :] = mb[0, rows, lo:lo + LANES].astype(jnp.float32)
            mf[c, 1, rows, :] = mb[1, rows, lo:lo + LANES].astype(jnp.float32)

    pieces = back_pieces(R)
    back = [[] for _ in pieces]
    for c in range(C):
        wide = slice(c * W, (c + 1) * W)
        for copy in copies[c]:
            copy.wait()

        @pl.loop(0, R // 8)
        def _(t):
            rows = pl.ds(pl.multiple_of(t * 8, 8), 8)
            values = [(recv[c, q, rows, 0:LANES], recv[c, q, rows, LANES:W]) for q in range(F)]
            for k, (re, im) in enumerate(block_dft(values, -1.0)):
                u[k, rows, 0:LANES] = re
                u[k, rows, LANES:W] = im

        @pl.loop(0, F)
        def _(k):
            cos, sin = square_tables(t_ref, k, C)
            part = halves(u[k])
            p = exact_dot(cos, part, ((1,), (0,)))
            q = exact_dot(sin, part, ((1,), (0,)))
            spec_re = p[:, 0:LANES] - q[:, LANES:]
            spec_im = p[:, LANES:] + q[:, 0:LANES]
            lines = pl.ds(k, A, stride=F)
            weight = wf[c, lines, :]
            res_re = weight * spec_re - mf[c, 0, lines, :]
            res_im = weight * spec_im - mf[c, 1, lines, :]
            part = halves(jnp.concatenate([res_re, res_im], axis=1))
            p = exact_dot(cos, part, ((0,), (0,)))
            q = exact_dot(sin, part, ((0,), (0,)))
            u[k, :, 0:LANES] = p[:, 0:LANES] + q[:, LANES:]
            u[k, :, LANES:W] = p[:, LANES:] - q[:, 0:LANES]

        for i, (start, size) in enumerate(pieces if c == C - 1 else [(0, R)]):

            @pl.loop(0, size // 8)
            def _(t):
                rows = pl.ds(pl.multiple_of(start + t * 8, 8), 8)
                values = [(u[k, rows, 0:LANES], u[k, rows, LANES:W]) for k in range(F)]
                for q, (re, im) in enumerate(block_dft(values, 1.0)):
                    sendy[q, rows, c * W:c * W + LANES] = re
                    sendy[q, rows, c * W + LANES:(c + 1) * W] = im

            span = pl.ds(start, size)
            for o in order:
                d = lax.rem(me + o, F)
                copy = pltpu.make_async_remote_copy(
                    src_ref=sendy.at[d, span, wide], dst_ref=recvy.at[me, span, wide],
                    send_sem=bs.at[c, i, o], recv_sem=br.at[c, i, o],
                    device_id={"facet": d}, device_id_type=pl.DeviceIdType.MESH,
                )
                copy.start()
                back[i].append(copy)
            copy = pltpu.make_async_copy(
                sendy.at[me, span, wide], recvy.at[me, span, wide], br.at[c, i, 0]
            )
            copy.start()
            back[i].append(copy)

        if c == 0:
            for copy in image_copies + halos:
                copy.wait()
            edges = [
                pltpu.make_async_copy(image_ref, image_hbm, in_sem.at[3]),
                pltpu.make_async_copy(up_ref, up_hbm, in_sem.at[4]),
                pltpu.make_async_copy(left_ref, left_hbm, in_sem.at[5]),
            ]
            for k in range(CH):
                first_up = jnp.where(me > 0, up_ref[k], 0.0)[7:8, :]
                first_left = jnp.where(mine > 0, left_ref[k], 0.0)[:, LANES - 1:LANES]
                p = dual[k, 0, 0:16, :].astype(jnp.float32)[0:8, :]
                q = dual[k, 1, 0:16, :].astype(jnp.float32)[0:8, :]
                lane = lax.broadcasted_iota(jnp.int32, (8, T), 1)
                q_prev = jnp.where(lane == 0, first_left[0:8, :], pltpu.roll(q, 1, 1))
                low[k] = image_ref[k, 0:8, :] - (first_up - p + q_prev - q)
                p = dual[k, 0, :, 0:LANES].astype(jnp.float32)
                q = dual[k, 1, :, 0:LANES].astype(jnp.float32)
                row = lax.broadcasted_iota(jnp.int32, (R, LANES), 0)
                p_prev = jnp.where(row == 0, first_up[:, 0:LANES], pltpu.roll(p, 1, 0))
                right[k] = image_ref[k, :, 0:LANES] - (p_prev - p + first_left - q)
            edges += [
                halo_copy(low, low_ref, hs.at[2], hr.at[2], {"facet": above}),
                halo_copy(right, right_ref, hs.at[3], hr.at[3], {"chan": before}),
            ]
            for copy in edges:
                copy.start()

    last = []
    for h, (start, size) in enumerate(pieces):
        for copy in back[h]:
            copy.wait()

        @pl.loop(0, size // 8)
        def _(t):
            rows = pl.ds(pl.multiple_of(start + t * 8, 8), 8)
            target = pl.ds(pl.multiple_of(t * 8, 8), 8)
            for c in range(C):
                re_at, im_at = pl.ds(c * W, LANES), pl.ds(c * W + LANES, LANES)
                values = [(recvy[j, rows, re_at], recvy[j, rows, im_at]) for j in range(F)]
                for b, (re, im) in enumerate(block_dft(values, 1.0)):
                    z[b, target, re_at] = re
                    z[b, target, im_at] = im

        span = pl.ds(start, size)

        @pl.loop(0, F)
        def _(b):
            line = exact_dot((t_ref[0, b], t_ref[1, b]), halves(z[b]), ((1,), (1,)))
            gt[pl.ds(b, A, stride=F), :] = line * scale

        for j in range(N // LANES):
            g[span, j * LANES:(j + 1) * LANES] = gt[j * LANES:(j + 1) * LANES, :].T[0:size, :]
        if h == 0:
            for o in range(CH):
                d = lax.rem(mine + o, CH)
                copy = halo_copy(
                    g.at[0:8, pl.ds(pl.multiple_of(d * T, LANES), T)], lowg_ref.at[mine],
                    gs.at[o], gr.at[o], {"chan": d, "facet": above},
                )
                copy.start()
                last.append(copy)
        for o in range(1, CH):
            d = lax.rem(mine + o, CH)
            e = lax.rem(mine + o + 1, CH)
            copy = halo_copy(
                g.at[span, pl.ds(pl.multiple_of(e * T, LANES), LANES)],
                rightg_ref.at[mine, span], rs.at[h, o], rr.at[h, o], {"chan": d},
            )
            copy.start()
            last.append(copy)
            copy = pltpu.make_async_remote_copy(
                src_ref=g.at[span, pl.ds(pl.multiple_of(d * T, LANES), T)],
                dst_ref=grad_ref.at[mine, span],
                send_sem=cs.at[h, o], recv_sem=cr.at[h, o],
                device_id={"chan": d}, device_id_type=pl.DeviceIdType.MESH,
            )
            copy.start()
            last.append(copy)
        copy = pltpu.make_async_copy(
            g.at[span, pl.ds(pl.multiple_of(mine * T, LANES), T)],
            grad_ref.at[mine, span], ls.at[1 + h],
        )
        copy.start()
        last.append(copy)
        copy = pltpu.make_async_copy(
            g.at[span, pl.ds(pl.multiple_of(after * T, LANES), LANES)],
            rightg_ref.at[mine, span], rr.at[h, 0],
        )
        copy.start()
        last.append(copy)
    for copy in edges + last:
        copy.wait()


def gradient_tiles(F, CH, image, weights, measured, dual):
    R, N = image.shape
    A = N // F
    C = A // LANES
    RC = R // LANES
    seed, turn = (jnp.asarray(t) for t in table_seeds(F, A))
    PC = len(back_pieces(R))
    T = N // CH
    tile = jax.ShapeDtypeStruct((CH, R, T), jnp.float32)
    line = jax.ShapeDtypeStruct((CH, 8, T), jnp.float32)
    side = jax.ShapeDtypeStruct((CH, R, LANES), jnp.float32)
    f32 = jnp.float32
    dma = pltpu.SemaphoreType.DMA
    vmem = pl.BlockSpec(memory_space=pltpu.VMEM)
    hbm = pl.BlockSpec(memory_space=pl.ANY)
    return pl.pallas_call(
        partial(kernel, F, CH),
        out_shape=(tile, tile, line, side, line, line, side, side),
        in_specs=[vmem, vmem, vmem, hbm, hbm, hbm],
        out_specs=(hbm,) * 8,
        scratch_shapes=[
            pltpu.VMEM((2, F, A, 2 * A), jnp.bfloat16),
            pltpu.VMEM((CH, R, T), f32),
            pltpu.VMEM((CH, 8, T), f32),
            pltpu.VMEM((CH, R, LANES), f32),
            pltpu.VMEM((CH, 2, R, T), jnp.bfloat16),
            pltpu.VMEM((CH, 8, T), f32),
            pltpu.VMEM((CH, R, LANES), f32),
            pltpu.VMEM((CH, 8, T), f32),
            pltpu.VMEM((CH, R, LANES), f32),
            pltpu.VMEM((RC, N, LANES), f32),
            pltpu.VMEM((F, LANES, 2 * A), f32),
            pltpu.VMEM((C, F, R, 2 * LANES), f32),
            pltpu.VMEM((C, F, R, 2 * LANES), f32),
            pltpu.VMEM((N, A), jnp.bfloat16),
            pltpu.VMEM((2, N, A), jnp.bfloat16),
            pltpu.VMEM((C, N, LANES), f32),
            pltpu.VMEM((C, 2, N, LANES), f32),
            pltpu.VMEM((F, A, 2 * LANES), f32),
            pltpu.VMEM((F, R, 2 * A), f32),
            pltpu.VMEM((F, R, 2 * A), f32),
            pltpu.VMEM((N, LANES), f32),
            pltpu.VMEM((R, N), f32),
            dma((6,)),
            dma((C, RC, F)), dma((C, RC, F)),
            dma((C, PC, F)), dma((C, PC, F)),
            dma((PC, CH)), dma((PC, CH)),
            dma((CH,)), dma((CH,)),
            dma((1 + PC,)),
            dma((4,)), dma((4,)),
            dma((PC, CH)), dma((PC, CH)),
            dma((CH,)), dma((CH,)),
        ],
        compiler_params=pltpu.CompilerParams(
            collective_id=0, has_side_effects=True, vmem_limit_bytes=60 * 1024 * 1024
        ),
    )(image, seed, turn, weights, measured, dual)


def prior_kernel(
    n, edge, x, g, d, up, left, low, lowg, right, rightg, image, dual, ext, held, carry, parts
):
    t = pl.program_id(0)
    CH, TR, T = x.shape
    now = lax.rem(t, 2)
    row = lax.broadcasted_iota(jnp.int32, (TR, T), 0)
    lane = lax.broadcasted_iota(jnp.int32, (TR, T), 1)

    @pl.when(t == 0)
    def _():
        carry[...] = jnp.where(edge[0] == 0, 0.0, up[...])

    @pl.when(t < n)
    def _():
        for c in range(CH):
            p = d[c, 0].astype(jnp.float32)
            q = d[c, 1].astype(jnp.float32)
            p_prev = jnp.where(row == 0, carry[c, 7:8, :], pltpu.roll(p, 1, 0))
            first = jnp.where(edge[2] == 0, 0.0, left[c])[:, LANES - 1:LANES]
            q_prev = jnp.where(lane == 0, first, pltpu.roll(q, 1, 1))
            adjoint = p_prev - p + q_prev - q
            value = x[c] - step_primal * (g[c] + adjoint)
            image[c] = value
            ext[now, c] = 2.0 * value - x[c]
            held[now, c, 0] = p
            held[now, c, 1] = q
            carry[c] = p[TR - 8:TR, :]

    @pl.when(t > 0)
    def _():
        was = 1 - now
        total = jnp.zeros((TR, T), jnp.float32)
        for c in range(CH):
            e = ext[was, c]
            beyond = jnp.where(edge[1] == 0, 0.0, low[c] - lowg[c])
            following = jnp.where(t < n, ext[now, c, 0:8, :], beyond)[0:1, :]
            rows = jnp.where(row == TR - 1, following, pltpu.roll(e, TR - 1, 0)) - e
            side = jnp.where(edge[3] == 0, 0.0, right[c] - rightg[c])[:, 0:1]
            cols = jnp.where(lane == T - 1, side, pltpu.roll(e, T - 1, 1)) - e
            first_part = held[was, c, 0] + step_dual * rows
            second_part = held[was, c, 1] + step_dual * cols
            parts[c, 0] = first_part
            parts[c, 1] = second_part
            total = total + (first_part * first_part + second_part * second_part)
        factor = 1.0 / jnp.maximum(1.0, jnp.sqrt(total) / clip_radius)
        for c in range(CH):
            dual[c, 0] = (parts[c, 0] * factor).astype(jnp.bfloat16)
            dual[c, 1] = (parts[c, 1] * factor).astype(jnp.bfloat16)


def prior(edge, x, g, dual, up, left, low, lowg, right, rightg):
    CH, R, T = x.shape
    TR = 64
    n = R // TR
    f32 = jnp.float32
    ahead = lambda t: jnp.minimum(t, n - 1)
    behind = lambda t: jnp.maximum(t - 1, 0)
    tile = pl.BlockSpec((CH, TR, T), lambda t: (0, ahead(t), 0))
    line = pl.BlockSpec((CH, 8, T), lambda t: (0, 0, 0))
    return pl.pallas_call(
        partial(prior_kernel, n),
        grid=(n + 1,),
        out_shape=(
            jax.ShapeDtypeStruct((CH, R, T), f32),
            jax.ShapeDtypeStruct((CH, 2, R, T), jnp.bfloat16),
        ),
        in_specs=[
            pl.BlockSpec(memory_space=pltpu.SMEM),
            tile,
            tile,
            pl.BlockSpec((CH, 2, TR, T), lambda t: (0, 0, ahead(t), 0)),
            line,
            pl.BlockSpec((CH, TR, LANES), lambda t: (0, ahead(t), 0)),
            line,
            line,
            pl.BlockSpec((CH, TR, LANES), lambda t: (0, behind(t), 0)),
            pl.BlockSpec((CH, TR, LANES), lambda t: (0, behind(t), 0)),
        ],
        out_specs=(tile, pl.BlockSpec((CH, 2, TR, T), lambda t: (0, 0, behind(t), 0))),
        scratch_shapes=[
            pltpu.VMEM((2, CH, TR, T), f32),
            pltpu.VMEM((2, CH, 2, TR, T), f32),
            pltpu.VMEM((CH, 8, T), f32),
            pltpu.VMEM((CH, 2, TR, T), f32),
        ],
        compiler_params=pltpu.CompilerParams(vmem_limit_bytes=60 * 1024 * 1024),
    )(edge, x, g, dual, up, left, low, lowg, right, rightg)


def shards(image_field, weights, measured, dual_field):
    F, CH = lax.axis_size("facet"), lax.axis_size("chan")
    tiles = gradient_tiles(F, CH, image_field[0], weights, measured, dual_field)
    f, c = lax.axis_index("facet"), lax.axis_index("chan")
    edge = jnp.stack([f > 0, f < F - 1, c > 0, c < CH - 1]).astype(jnp.int32)
    return prior(edge, tiles[0], tiles[1], dual_field, *tiles[2:])


def solution(mesh):
    placed = (
        P("chan", "facet", None),
        P("chan", None, "facet"),
        P("chan", None, None, "facet"),
        P(None, None, "facet", "chan"),
    )
    return jax.shard_map(
        shards,
        mesh=mesh,
        in_specs=placed,
        out_specs=(P(None, "facet", "chan"), P(None, None, "facet", "chan")),
        check_vma=False,
    )
```
